32 devices in a mesh: group: 2 (over x), region: 8 (over z, y), window: 2 (over core).
Axes of the slice: x: 2, y: 2, z: 4, core: 2. Of those that a mesh axis runs over, the one named last changes fastest.
Arguments:
- flux: bfloat16 [32, 4096, 128], P(('group', 'window'), 'region'), parts along dimension 0, may hold values from -6 to 6
- blend: float32 [16, 16], replicated
- footprints: bfloat16 [4, 8192, 4096], P(('group', 'window'), 'region'), parts along dimension 0, may hold values from -0.03125 to 0.03125
- receptor_block: int32 [4, 8192], P(('group', 'window'), 'region'), parts along dimension 0, may hold values from 0 to 15, as said below
- cell_block: int32 [4, 8192], P(('group', 'window'), 'region'), parts along dimension 0, may hold values from 0 to 7
- slice_index: int32 [4, 8192], P(('group', 'window'), 'region'), parts along dimension 0, may hold values from 0 to 15
- live_counts: int32 [4, 8], P(('group', 'window'), 'region'), parts along dimension 0, may hold values from 16 to 1024, as said below
- observed: bfloat16 [4, 1024, 128], P(('group', 'window'), 'region'), parts along dimension 0, may hold values from -3 to 3
- inv_var: float32 [4, 1024], P(('group', 'window'), 'region'), parts along dimension 0, may hold values from 0.5 to 2
- prior_mix: bfloat16 [128, 128], replicated, may hold values from -2 to 2
Outputs:
- misfit: bfloat16 [4, 1024, 128], P(('group', 'window'), 'region'), parts along dimension 0
- gradient: bfloat16 [32, 4096, 128], P(('group', 'window'), 'region'), parts along dimension 0
The draws below stay inside these ranges and needn't reach their ends.
There are 2 independent parts, one for each index of `group`. The reference program is written for one: setup_inputs(seed, part) draws one part's arguments, and reference() takes and returns one part's arrays. A program takes and returns all parts, laid end to end along the dimension named above; an argument that names none is the same for every part. Nothing has to cross between parts.
Inputs may be any that keep to these rules, and one draw needn't show every extreme that they name: `receptor_block`: receptor blocks j * 2 to (j + 1) * 2 - 1 of a window belong to region j. Of the 1024 slots of one window and region, the first live_counts entries are footprint blocks and the rest are unused. The live blocks of one window and region name at most 2 distinct receptor blocks of any one region, and in every draw, for each window, some region has 2 of its receptor blocks named by the live blocks of every region. `live_counts`: some window and region has all 1024 slots live.
All inputs are finite; a program needn't handle non-finite values.
Results may differ from the reference program's by a relative error of at most 0.018.
Values may be sent and summed in bfloat16 or wider, within the bound.
A program may use at most 192 MiB of HBM per device.

```python
import math
import jax
import jax.numpy as jnp
from jax import lax

ENS = 128
BLOCK = 64
CAP = 2
RB_DEV = 2
CB_DEV = 8
NB = 1024
SLICES = 16
NWIN = 2
REGIONS = 8
RB_WIN = 16
REC_WIN = 1024
CELLS = 4096
NBLK = 8192


def draw_blend(key, part):
    slot_ids = jnp.arange(SLICES)
    distance = jnp.abs(slot_ids[:, None] - slot_ids[None, :]).astype(jnp.float32)
    diagonal_part = jax.random.uniform(jax.random.fold_in(key, 5101), (SLICES, SLICES), jnp.float32, 0.6, 1.0)
    side_part = jax.random.uniform(jax.random.fold_in(key, 5102), (SLICES, SLICES), jnp.float32, -1.0, 1.0)
    decay_span = max(SLICES // 4, 1)
    return jnp.where(distance == 0.0, diagonal_part, 0.4 * side_part * jnp.exp(-distance / decay_span))


def block_plan(key):
    sub_keys = [jax.random.fold_in(key, 9100 + number) for number in range(8)]
    live_least = REGIONS * CAP
    draw_one = jax.random.randint(sub_keys[0], (NWIN, REGIONS), 0, 16)
    draw_two = jax.random.randint(sub_keys[1], (NWIN, REGIONS), 0, 16)
    counts = live_least + (NB - live_least) * draw_one * draw_two // 225
    busiest = jax.random.randint(sub_keys[2], (), 0, NWIN * REGIONS)
    counts = jnp.where(jnp.arange(NWIN * REGIONS).reshape(NWIN, REGIONS) == busiest, NB, counts)
    picked = jax.random.randint(sub_keys[3], (NWIN, REGIONS, REGIONS), 1, CAP + 1)
    fullest = jax.random.randint(sub_keys[4], (NWIN, 1, 1), 0, REGIONS)
    picked = jnp.where(jnp.arange(REGIONS)[None, None, :] == fullest, CAP, picked)
    scores = jax.random.randint(sub_keys[5], (NWIN, REGIONS, REGIONS, RB_DEV), 0, 1 << 20) * RB_DEV + jnp.arange(RB_DEV)
    ranking = jnp.argsort(scores, axis=-1)[..., :CAP]
    owners = jnp.arange(REGIONS)[None, None, :, None] * RB_DEV + ranking
    usable = jnp.arange(CAP)[None, None, None, :] < picked[..., None]
    owners = owners.reshape(NWIN, REGIONS, REGIONS * CAP)
    usable = usable.reshape(NWIN, REGIONS, REGIONS * CAP).astype(jnp.int32)
    position = jnp.cumsum(usable, axis=-1) - usable
    spot_ids = jnp.arange(REGIONS * CAP)
    matches = (position[..., None, :] == spot_ids[:, None]) & (usable[..., None, :] > 0)
    listed = jnp.sum(jnp.where(matches, owners[..., None, :], 0), axis=-1)
    touched = jnp.sum(usable, axis=-1)
    item_ids = jnp.arange(NB)
    spare_pick = jax.random.randint(sub_keys[6], (NWIN, REGIONS, NB), 0, touched[..., None])
    chosen = jnp.where(item_ids < touched[..., None], item_ids, spare_pick)
    targets = jnp.take_along_axis(listed, chosen, axis=-1)
    shuffle = jnp.where(item_ids < counts[..., None], jax.random.randint(sub_keys[7], (NWIN, REGIONS, NB), 0, 1 << 20) * NB + item_ids, (1 << 30) + item_ids)
    slot_order = jnp.argsort(shuffle, axis=-1)
    receptor_ids = jnp.take_along_axis(targets, slot_order, axis=-1)
    return (counts.astype(jnp.int32), receptor_ids.reshape(NWIN, REGIONS * NB).astype(jnp.int32))


def draw_receptor_block(key, part):
    counts, receptor_ids = block_plan(key)
    return receptor_ids


def draw_live_counts(key, part):
    counts, receptor_ids = block_plan(key)
    return counts


def touch_ends(array, stream_key, smallest, high):
    place = [jax.random.randint(jax.random.fold_in(stream_key, axis), (), 0, length) for axis, length in enumerate(array.shape)]
    main_axis = array.shape.index(max(array.shape))
    neighbour = place[:main_axis] + [(place[main_axis] + 1) % array.shape[main_axis]] + place[main_axis + 1:]
    return array.at[tuple(place)].set(smallest).at[tuple(neighbour)].set(high)


def block_levels(stream_key, dims, shards, smallest, top_value):
    def one(axis_at, shards_of):
        heights = jax.random.uniform(jax.random.fold_in(jax.random.fold_in(stream_key, 6), axis_at), (shards_of,), jnp.float32, smallest / len(shards), top_value / len(shards))
        return jnp.repeat(jnp.exp(heights), dims[axis_at] // shards_of).reshape((-1,) + (1,) * (len(dims) - axis_at - 1))

    level = one(*shards[0])
    for cut in shards[1:]:
        level = level * one(*cut)
    return level


def scatter_about(own_key, shape, deviation, most, shards=(), held_as=jnp.bfloat16):
    array = deviation * jax.random.normal(own_key, shape, jnp.float32)
    if shards:
        array = array * block_levels(own_key, shape, shards, -0.22, 0.18)
    return jnp.clip(array, -most, most).astype(held_as)


def setup_inputs(seed: int = 0, part: int = 0) -> dict:
    splits = jax.random.split(jax.random.key(seed), 11)
    part_keys = jax.random.split(jax.random.fold_in(splits[10], part), 11)
    return {
        "flux": scatter_about(part_keys[0], (SLICES, CELLS, ENS), 1.0, 6.0, ((0, 2), (1, 8))),
        "blend": draw_blend(jax.random.fold_in(splits[10], 71), part),
        "footprints": scatter_about(part_keys[2], (NWIN, NBLK, BLOCK * BLOCK), (BLOCK * NB // RB_DEV) ** -0.5, 0.03125, ((0, 2), (1, 8))),
        "receptor_block": draw_receptor_block(jax.random.fold_in(jax.random.fold_in(splits[10], part), 71), part),
        "cell_block": touch_ends(jax.random.randint(part_keys[4], (NWIN, NBLK), 0, CB_DEV), jax.random.fold_in(part_keys[4], 1), 0, CB_DEV - 1).astype(jnp.int32),
        "slice_index": touch_ends(jax.random.randint(part_keys[5], (NWIN, NBLK), 0, SLICES), jax.random.fold_in(part_keys[5], 1), 0, SLICES - 1).astype(jnp.int32),
        "live_counts": draw_live_counts(jax.random.fold_in(jax.random.fold_in(splits[10], part), 71), part),
        "observed": scatter_about(part_keys[7], (NWIN, REC_WIN, ENS), 0.5, 3.0, ((0, 2), (1, 8))),
        "inv_var": jnp.clip(jnp.exp(math.log(2.0) - 1.3862944 * jax.random.uniform(part_keys[8], (NWIN, REC_WIN), jnp.float32) ** block_levels(part_keys[8], (NWIN, REC_WIN), ((0, 2), (1, 8)), -0.2, 0.2)), 0.5, 2.0),
        "prior_mix": scatter_about(splits[9], (ENS, ENS), (ENS // 16) ** -0.5, 2.0),
    }


def reference(flux, blend, footprints, receptor_block, cell_block, slice_index, live_counts, observed, inv_var, prior_mix):
    highest = lax.Precision.HIGHEST
    blended = jnp.einsum("ts,sce->tce", blend, flux.astype(jnp.float32), precision=highest).astype(jnp.bfloat16)
    global_blocks = CELLS // BLOCK
    panels = blended.reshape(SLICES * global_blocks, BLOCK, ENS)
    device_count = NWIN * REGIONS
    footprint_sets = footprints.reshape(device_count, NB, BLOCK, BLOCK)
    receptor_sets = receptor_block.reshape(device_count, NB)
    cell_sets = cell_block.reshape(device_count, NB)
    slice_sets = slice_index.reshape(device_count, NB)
    live_sets = jnp.arange(NB, dtype=jnp.int32)[None, :] < live_counts.reshape(device_count)[:, None]
    region_ids = (jnp.arange(device_count, dtype=jnp.int32) % REGIONS).astype(jnp.int32)
    window_ids = (jnp.arange(device_count, dtype=jnp.int32) // REGIONS).astype(jnp.int32)
    panel_sets = (slice_sets * global_blocks + region_ids[:, None] * CB_DEV + cell_sets).astype(jnp.int32)
    receptor_rows = (window_ids[:, None] * RB_WIN + receptor_sets).astype(jnp.int32)
    items = (footprint_sets, receptor_rows, panel_sets, live_sets)

    def forward(totals, item):
        footprint_set, receptor_row, panel_set, live_set = item
        gathered = panels[panel_set]
        products = jnp.einsum("kab,kbe->kae", footprint_set.astype(jnp.float32), gathered.astype(jnp.float32))
        products = jnp.where(live_set[:, None, None], products, jnp.zeros_like(products))
        return totals.at[receptor_row].add(products), None

    evolved, unused = lax.scan(forward, jnp.zeros((NWIN * RB_WIN, BLOCK, ENS), jnp.float32), items)
    weights_here = inv_var.reshape(NWIN * RB_WIN, BLOCK)[:, :, None]
    observed_here = observed.reshape(NWIN * RB_WIN, BLOCK, ENS).astype(jnp.float32)
    misfit = (weights_here * (evolved - observed_here)).astype(jnp.bfloat16)

    def adjoint(totals, item):
        footprint_set, receptor_row, panel_set, live_set = item
        rows_here = misfit[receptor_row]
        pulled_back = jnp.einsum("kab,kae->kbe", footprint_set.astype(jnp.float32), rows_here.astype(jnp.float32))
        pulled_back = jnp.where(live_set[:, None, None], pulled_back, jnp.zeros_like(pulled_back))
        return totals.at[panel_set].add(pulled_back), None

    collected, unused_two = lax.scan(adjoint, jnp.zeros((SLICES * global_blocks, BLOCK, ENS), jnp.float32), items)
    collected = collected.reshape(SLICES, CELLS, ENS)
    pulled = jnp.einsum("ts,tce->sce", blend, collected, precision=highest).astype(jnp.bfloat16)
    gradient = jnp.dot(pulled.reshape(SLICES * CELLS, ENS), prior_mix, preferred_element_type=jnp.float32)
    gradient = gradient.astype(jnp.bfloat16).reshape(SLICES, CELLS, ENS)
    return misfit.reshape(NWIN, REC_WIN, ENS), gradient
```

```python
import functools

import jax
import jax.numpy as jnp
from jax import lax
from jax.experimental import pallas as pl
from jax.experimental.pallas import tpu as pltpu
from jax.sharding import PartitionSpec as P

BLOCK = 64
MESH = pl.DeviceIdType.MESH
F32 = jnp.float32
BF16 = jnp.bfloat16
STEP = 128
SUB = 16
CELLS_AT_ONCE = 16
PIECES = 4


def spread(matrix, width):
    size = matrix.shape[0]
    full = size * width
    row = lax.broadcasted_iota(jnp.int32, (full, size), 0)
    col = lax.broadcasted_iota(jnp.int32, (full, size), 1)
    pick = (row // width == col).astype(BF16)
    row_f = lax.broadcasted_iota(jnp.int32, (full, full), 0)
    col_f = lax.broadcasted_iota(jnp.int32, (full, full), 1)
    same = row_f % width == col_f % width
    high = matrix.astype(BF16)
    low = (matrix - high.astype(F32)).astype(BF16)
    parts = []
    for part in (high, low):
        tall = jnp.dot(pick, part, preferred_element_type=F32).astype(BF16)
        wide = lax.dot_general(tall, pick, (((1,), (1,)), ((), ())), preferred_element_type=F32)
        parts.append(jnp.where(same, wide, 0.0).astype(BF16))
    return parts


def blend_kernel(blend_ref, flux_ref, panels_ref, full, local_sem, send_sem, recv_sem):
    me = lax.axis_index("window")
    other = 1 - me
    slabs, cells, ens = flux_ref.shape
    slices = panels_ref.shape[0]
    barrier = pltpu.get_barrier_semaphore()
    pl.semaphore_signal(barrier, inc=1, device_id={"window": other}, device_id_type=MESH)
    piece = cells // PIECES
    locals_, sends = [], []
    for k in range(PIECES):
        span = pl.ds(k * piece, piece)
        locals_.append(
            pltpu.make_async_copy(
                flux_ref.at[:, span, :], full.at[pl.ds(me * slabs, slabs), span, :], local_sem.at[k]
            )
        )
        locals_[-1].start()
    pl.semaphore_wait(barrier, 1)
    for k in range(PIECES):
        span = pl.ds(k * piece, piece)
        sends.append(
            pltpu.make_async_remote_copy(
                src_ref=flux_ref.at[:, span, :],
                dst_ref=full.at[pl.ds(me * slabs, slabs), span, :],
                send_sem=send_sem.at[k],
                recv_sem=recv_sem.at[k],
                device_id={"window": other},
                device_id_type=MESH,
            )
        )
        sends[-1].start()
    high, low = spread(blend_ref[...], CELLS_AT_ONCE)
    for k in range(PIECES):
        locals_[k].wait()
        sends[k].wait_recv()

        def group(g, carry, k=k):
            sides = []
            for half in range(2):
                start = pl.multiple_of(k * piece + g * 2 * CELLS_AT_ONCE + half * CELLS_AT_ONCE, CELLS_AT_ONCE)
                sides.append(full[:, pl.ds(start, CELLS_AT_ONCE), :].reshape(slices * CELLS_AT_ONCE, ens))
            rhs = jnp.concatenate(sides, axis=1)
            out = jnp.dot(high, rhs, preferred_element_type=F32) + jnp.dot(low, rhs, preferred_element_type=F32)
            out = out.astype(BF16)
            for half in range(2):
                start = pl.multiple_of(k * piece + g * 2 * CELLS_AT_ONCE + half * CELLS_AT_ONCE, CELLS_AT_ONCE)
                panels_ref[:, pl.ds(start, CELLS_AT_ONCE), :] = out[:, half * ens : (half + 1) * ens].reshape(
                    slices, CELLS_AT_ONCE, ens
                )
            return carry

        lax.fori_loop(0, piece // (2 * CELLS_AT_ONCE), group, 0, unroll=2)
    for k in range(PIECES):
        sends[k].wait_send()


def split_rows(f):
    lower = lax.broadcasted_iota(jnp.int32, f.shape, 1) < BLOCK
    zero = jnp.zeros_like(f)
    return jnp.concatenate([jnp.where(lower, f, zero), jnp.where(lower, zero, f)], axis=0)


def forward_kernel(to_ref, from_ref, fp_ref, panels_ref, frel_ref, part_ref, acc):
    step = pl.program_id(0)
    count = part_ref.shape[0]

    @pl.when(step == 0)
    def _():
        acc[...] = jnp.zeros_like(acc)

    def body(g, carry):
        base = pl.multiple_of(g * SUB, SUB)
        x = fp_ref[pl.ds(base, SUB), :].reshape(SUB, BLOCK // 2, 2 * BLOCK)
        frel_ref[pl.ds(base, SUB)] = x
        for j in range(SUB):
            slot = step * STEP + base + j
            p = panels_ref[from_ref[slot]]
            d = jnp.dot(split_rows(x[j]), jnp.concatenate([p, p], axis=0), preferred_element_type=F32)
            q = to_ref[slot]
            acc[q] += d
        return carry

    lax.fori_loop(0, STEP // SUB, body, 0)

    @pl.when(step == pl.num_programs(0) - 1)
    def _():
        part_ref[...] = acc[pl.ds(0, count)].astype(BF16)


def exchange_kernel(regions, part_ref, obs_ref, inv_ref, all_ref, own_ref, got, send_a, recv_a, send_b, recv_b):
    me = lax.axis_index("region")
    rows, ens = obs_ref.shape
    barrier = pltpu.get_barrier_semaphore()
    for k in range(1, regions):
        peer = lax.rem(me + k, regions)
        pl.semaphore_signal(barrier, inc=1, device_id={"region": peer}, device_id_type=MESH)
    row = lax.broadcasted_iota(jnp.int32, (rows, rows), 0)
    col = lax.broadcasted_iota(jnp.int32, (rows, rows), 1)
    inner = row % BLOCK
    half = BLOCK // 2
    picked = (row // BLOCK) * BLOCK + (inner % half) * 2 + inner // half == col
    table = picked.astype(BF16)
    obs = jnp.dot(table, obs_ref[...], preferred_element_type=F32)
    inv = jnp.sum(jnp.where(picked, inv_ref[...], 0.0), axis=1, keepdims=True)
    pl.semaphore_wait(barrier, regions - 1)

    def first(k):
        peer = lax.rem(me + k, regions)
        return pltpu.make_async_remote_copy(
            src_ref=part_ref.at[peer],
            dst_ref=got.at[k],
            send_sem=send_a.at[k],
            recv_sem=recv_a.at[k],
            device_id={"region": peer},
            device_id_type=MESH,
        )

    def second(k):
        peer = lax.rem(me + k, regions)
        return pltpu.make_async_remote_copy(
            src_ref=all_ref.at[me],
            dst_ref=all_ref.at[me],
            send_sem=send_b.at[k],
            recv_sem=recv_b.at[k],
            device_id={"region": peer},
            device_id_type=MESH,
        )

    firsts = [first(k) for k in range(1, regions)]
    for copy in firsts:
        copy.start()
    evolved = part_ref[me].astype(F32)
    for k in range(1, regions):
        firsts[k - 1].wait_recv()
        evolved = evolved + got[k].astype(F32)
    misfit = (inv * (evolved - obs)).astype(BF16)
    all_ref[me] = misfit
    seconds = [second(k) for k in range(1, regions)]
    for copy in seconds:
        copy.start()
    own_ref[...] = lax.dot_general(
        table, misfit, (((0,), (0,)), ((), ())), preferred_element_type=F32
    ).astype(BF16)
    for copy in firsts:
        copy.wait_send()
    for k in range(1, regions):
        source = lax.rem(me - k + regions, regions)
        pltpu.make_async_remote_copy(
            src_ref=all_ref.at[source],
            dst_ref=all_ref.at[source],
            send_sem=send_b.at[k],
            recv_sem=recv_b.at[k],
            device_id={"region": source},
            device_id_type=MESH,
        ).wait_recv()
    for copy in seconds:
        copy.wait_send()


def adjoint_kernel(to_ref, from_ref, blend_ref, frel_ref, misfit_ref, pulled_ref, acc):
    step = pl.program_id(0)
    slices, cells, ens = pulled_ref.shape

    @pl.when(step == 0)
    def _():
        acc[...] = jnp.zeros_like(acc)

    def body(g, carry):
        base = pl.multiple_of(g * SUB, SUB)
        for j in range(SUB):
            slot = step * STEP + base + j
            m = misfit_ref[from_ref[slot]]
            d = lax.dot_general(
                split_rows(frel_ref[base + j]), m, (((0,), (0,)), ((), ())), preferred_element_type=F32
            )
            p = to_ref[slot]
            acc[p] += d[:BLOCK] + d[BLOCK:]
        return carry

    lax.fori_loop(0, STEP // SUB, body, 0)

    @pl.when(step == pl.num_programs(0) - 1)
    def _():
        high, low = spread(blend_ref[...], CELLS_AT_ONCE)
        blocks = cells // BLOCK
        shape = (slices * CELLS_AT_ONCE, ens)

        def group(g, carry):
            block = g // (BLOCK // (2 * CELLS_AT_ONCE))
            within = g % (BLOCK // (2 * CELLS_AT_ONCE))
            sides = []
            for half in range(2):
                start = pl.multiple_of(within * 2 * CELLS_AT_ONCE + half * CELLS_AT_ONCE, CELLS_AT_ONCE)
                rows = [acc[t * blocks + block, pl.ds(start, CELLS_AT_ONCE), :] for t in range(slices)]
                sides.append(jnp.concatenate(rows, axis=0))
            rhs = jnp.concatenate(sides, axis=1)
            rhs_high = rhs.astype(BF16)
            rhs_low = (rhs - rhs_high.astype(F32)).astype(BF16)
            dims = (((0,), (0,)), ((), ()))
            out = lax.dot_general(high, rhs_high, dims, preferred_element_type=F32)
            out = out + lax.dot_general(low, rhs_high, dims, preferred_element_type=F32)
            out = (out + lax.dot_general(high, rhs_low, dims, preferred_element_type=F32)).astype(BF16)
            for half in range(2):
                start = pl.multiple_of((g * 2 + half) * CELLS_AT_ONCE, CELLS_AT_ONCE)
                pulled_ref[:, pl.ds(start, CELLS_AT_ONCE), :] = out[:, half * ens : (half + 1) * ens].reshape(
                    slices, CELLS_AT_ONCE, ens
                )
            return carry

        lax.fori_loop(0, cells // (2 * CELLS_AT_ONCE), group, 0)


def gradient_kernel(pulled_ref, mix_ref, grad_ref, got, send_sem, recv_sem):
    me = lax.axis_index("window")
    other = 1 - me
    slabs, cells, ens = grad_ref.shape
    barrier = pltpu.get_barrier_semaphore()
    pl.semaphore_signal(barrier, inc=1, device_id={"window": other}, device_id_type=MESH)
    pl.semaphore_wait(barrier, 1)
    sends = []
    for k in range(slabs):
        sends.append(
            pltpu.make_async_remote_copy(
                src_ref=pulled_ref.at[other * slabs + k],
                dst_ref=got.at[k],
                send_sem=send_sem.at[k],
                recv_sem=recv_sem.at[k],
                device_id={"window": other},
                device_id_type=MESH,
            )
        )
        sends[-1].start()
    mix = mix_ref[...]
    for k in range(slabs):
        sends[k].wait_recv()
        total = (pulled_ref[me * slabs + k].astype(F32) + got[k].astype(F32)).astype(BF16)
        grad_ref[k] = jnp.dot(total, mix, preferred_element_type=F32).astype(BF16)
    for k in range(slabs):
        sends[k].wait_send()


def vmem():
    return pl.BlockSpec(memory_space=pltpu.VMEM)


def shards(
    regions,
    flux,
    blend,
    footprints,
    receptor_block,
    cell_block,
    slice_index,
    live_counts,
    observed,
    inv_var,
    prior_mix,
):
    slabs, cells, ens = flux.shape
    slices = blend.shape[0]
    cell_blocks = cells // BLOCK
    panel_total = slices * cell_blocks
    slots = footprints.shape[1]
    rows = observed.shape[1]
    own_blocks = rows // BLOCK
    window_blocks = own_blocks * regions

    live = jnp.arange(slots) < live_counts[0, 0]
    panel_ids = slice_index[0] * cell_blocks + cell_block[0]
    receptor_to = jnp.where(live, receptor_block[0], window_blocks)
    receptor_from = jnp.where(live, receptor_block[0], 0)
    panel_to = jnp.where(live, panel_ids, panel_total)
    panel_from = jnp.where(live, panel_ids, 0)

    panels = pl.pallas_call(
        blend_kernel,
        out_shape=jax.ShapeDtypeStruct((slices, cells, ens), BF16),
        in_specs=[vmem(), pl.BlockSpec(memory_space=pl.ANY)],
        out_specs=vmem(),
        scratch_shapes=[
            pltpu.VMEM((slices, cells, ens), BF16),
            pltpu.SemaphoreType.DMA((PIECES,)),
            pltpu.SemaphoreType.DMA((PIECES,)),
            pltpu.SemaphoreType.DMA((PIECES,)),
        ],
        compiler_params=pltpu.CompilerParams(collective_id=0, has_side_effects=True, vmem_limit_bytes=32 << 20),
        name="blend_slices",
    )(blend, flux)

    frel, part = pl.pallas_call(
        forward_kernel,
        out_shape=(
            jax.ShapeDtypeStruct((slots, BLOCK // 2, 2 * BLOCK), BF16),
            jax.ShapeDtypeStruct((window_blocks, BLOCK, ens), BF16),
        ),
        grid_spec=pltpu.PrefetchScalarGridSpec(
            num_scalar_prefetch=2,
            grid=(slots // STEP,),
            in_specs=[
                pl.BlockSpec((STEP, BLOCK * BLOCK), lambda i, a, b: (i, 0)),
                pl.BlockSpec((panel_total, BLOCK, ens), lambda i, a, b: (0, 0, 0)),
            ],
            out_specs=[
                pl.BlockSpec((STEP, BLOCK // 2, 2 * BLOCK), lambda i, a, b: (i, 0, 0)),
                pl.BlockSpec((window_blocks, BLOCK, ens), lambda i, a, b: (0, 0, 0)),
            ],
            scratch_shapes=[pltpu.VMEM((window_blocks + 1, BLOCK, ens), F32)],
        ),
        compiler_params=pltpu.CompilerParams(vmem_limit_bytes=32 << 20),
        name="forward_blocks",
    )(receptor_to, panel_from, footprints[0], panels.reshape(panel_total, BLOCK, ens))

    misfit_all, misfit = pl.pallas_call(
        functools.partial(exchange_kernel, regions),
        out_shape=(
            jax.ShapeDtypeStruct((regions, rows, ens), BF16),
            jax.ShapeDtypeStruct((rows, ens), BF16),
        ),
        in_specs=[vmem()] * 3,
        out_specs=(vmem(), vmem()),
        scratch_shapes=[
            pltpu.VMEM((regions, rows, ens), BF16),
            pltpu.SemaphoreType.DMA((regions,)),
            pltpu.SemaphoreType.DMA((regions,)),
            pltpu.SemaphoreType.DMA((regions,)),
            pltpu.SemaphoreType.DMA((regions,)),
        ],
        compiler_params=pltpu.CompilerParams(collective_id=1, has_side_effects=True, vmem_limit_bytes=32 << 20),
        name="misfit_exchange",
    )(part.reshape(regions, rows, ens), observed[0], inv_var)

    pulled = pl.pallas_call(
        adjoint_kernel,
        out_shape=jax.ShapeDtypeStruct((slices, cells, ens), BF16),
        grid_spec=pltpu.PrefetchScalarGridSpec(
            num_scalar_prefetch=2,
            grid=(slots // STEP,),
            in_specs=[
                pl.BlockSpec((slices, slices), lambda i, a, b: (0, 0)),
                pl.BlockSpec((STEP, BLOCK // 2, 2 * BLOCK), lambda i, a, b: (i, 0, 0)),
                pl.BlockSpec((window_blocks, BLOCK, ens), lambda i, a, b: (0, 0, 0)),
            ],
            out_specs=pl.BlockSpec((slices, cells, ens), lambda i, a, b: (0, 0, 0)),
            scratch_shapes=[pltpu.VMEM((panel_total + 1, BLOCK, ens), F32)],
        ),
        compiler_params=pltpu.CompilerParams(vmem_limit_bytes=32 << 20),
        name="adjoint_blocks",
    )(panel_to, receptor_from, blend, frel, misfit_all.reshape(window_blocks, BLOCK, ens))

    gradient = pl.pallas_call(
        gradient_kernel,
        out_shape=jax.ShapeDtypeStruct((slabs, cells, ens), BF16),
        in_specs=[vmem(), vmem()],
        out_specs=vmem(),
        scratch_shapes=[
            pltpu.VMEM((slabs, cells, ens), BF16),
            pltpu.SemaphoreType.DMA((slabs,)),
            pltpu.SemaphoreType.DMA((slabs,)),
        ],
        compiler_params=pltpu.CompilerParams(collective_id=2, has_side_effects=True, vmem_limit_bytes=32 << 20),
        name="gradient_exchange",
    )(pulled, prior_mix)
    return misfit[None], gradient


def solution(mesh):
    in_specs = (
        P(("group", "window"), "region", None),
        P(),
        P(("group", "window"), "region", None),
        P(("group", "window"), "region"),
        P(("group", "window"), "region"),
        P(("group", "window"), "region"),
        P(("group", "window"), "region"),
        P(("group", "window"), "region", None),
        P(("group", "window"), "region"),
        P(),
    )
    out_specs = (P(("group", "window"), "region", None), P(("group", "window"), "region", None))
    return jax.shard_map(
        functools.partial(shards, mesh.shape["region"]),
        mesh=mesh,
        in_specs=in_specs,
        out_specs=out_specs,
        check_vma=False,
    )
```

```python
import functools

import jax
import jax.numpy as jnp
from jax import lax
from jax.experimental import pallas as pl
from jax.experimental.pallas import tpu as pltpu
from jax.sharding import PartitionSpec as P

BLOCK = 64
MESH = pl.DeviceIdType.MESH
F32 = jnp.float32
BF16 = jnp.bfloat16
SUB = 16
CELLS_AT_ONCE = 16
PIECES = 4
LOADS = 8
PAIRS = 8
TURNS = 8
LAG = 2


def spread(matrix, width):
    size = matrix.shape[0]
    full = size * width
    row = lax.broadcasted_iota(jnp.int32, (full, size), 0)
    col = lax.broadcasted_iota(jnp.int32, (full, size), 1)
    pick = (row // width == col).astype(BF16)
    row_f = lax.broadcasted_iota(jnp.int32, (full, full), 0)
    col_f = lax.broadcasted_iota(jnp.int32, (full, full), 1)
    same = row_f % width == col_f % width
    high = matrix.astype(BF16)
    low = (matrix - high.astype(F32)).astype(BF16)
    parts = []
    for part in (high, low):
        tall = jnp.dot(pick, part, preferred_element_type=F32).astype(BF16)
        wide = lax.dot_general(tall, pick, (((1,), (1,)), ((), ())), preferred_element_type=F32)
        parts.append(jnp.where(same, wide, 0.0).astype(BF16))
    return parts


def halves_swapped(x):
    return pltpu.roll(x, BLOCK, 1)


def blend_kernel(
    window_blocks,
    recv_ref,
    cell_ref,
    slice_ref,
    live_ref,
    blend_hbm,
    flux_hbm,
    fp_hbm,
    panels_ref,
    pairs_ref,
    index_ref,
    full,
    raw,
    blend_ref,
    blend_sem,
    fp_sem,
    local_sem,
    send_sem,
    recv_sem,
):
    me = lax.axis_index("window")
    other = 1 - me
    slabs, cells, ens = flux_hbm.shape
    slices = panels_ref.shape[0]
    slots = raw.shape[0]
    barrier = pltpu.get_barrier_semaphore()
    pl.semaphore_signal(barrier, inc=1, device_id={"window": other}, device_id_type=MESH)
    blend_copy = pltpu.make_async_copy(blend_hbm, blend_ref, blend_sem)
    blend_copy.start()
    piece = cells // PIECES
    locals_, sends, loads = [], [], []
    for k in range(PIECES):
        span = pl.ds(k * piece, piece)
        locals_.append(
            pltpu.make_async_copy(
                flux_hbm.at[:, span, :], full.at[pl.ds(me * slabs, slabs), span, :], local_sem.at[k]
            )
        )
        locals_[-1].start()
    part = slots // LOADS
    for k in range(LOADS):
        span = pl.ds(k * part, part)
        loads.append(pltpu.make_async_copy(fp_hbm.at[0, span, :], raw.at[span, :], fp_sem.at[k]))
    loads[0].start()
    pl.semaphore_wait(barrier, 1)
    for k in range(PIECES):
        span = pl.ds(k * piece, piece)
        sends.append(
            pltpu.make_async_remote_copy(
                src_ref=flux_hbm.at[:, span, :],
                dst_ref=full.at[pl.ds(me * slabs, slabs), span, :],
                send_sem=send_sem.at[k],
                recv_sem=recv_sem.at[k],
                device_id={"window": other},
                device_id_type=MESH,
            )
        )
        sends[-1].start()
    for k in range(1, LOADS):
        loads[k].start()

    cell_blocks = cells // BLOCK
    live = lax.broadcasted_iota(jnp.int32, recv_ref.shape, 1) < live_ref[...]
    panel = slice_ref[...] * cell_blocks + cell_ref[...]
    index_ref[pl.ds(0, 1), :] = jnp.where(live, recv_ref[...], window_blocks)
    index_ref[pl.ds(1, 1), :] = jnp.where(live, panel, 0)
    index_ref[pl.ds(2, 1), :] = jnp.where(live, panel, slices * cell_blocks)
    index_ref[pl.ds(3, 1), :] = jnp.where(live, recv_ref[...], 0)
    blend_copy.wait()
    high, low = spread(blend_ref[...], CELLS_AT_ONCE)

    def arrange(k):
        loads[k].wait()

        def body(g, carry):
            base = pl.multiple_of(k * part + g * SUB, SUB)
            x = raw[pl.ds(base, SUB), :].reshape(SUB, BLOCK // 2, 2 * BLOCK)
            lower = lax.broadcasted_iota(jnp.int32, (BLOCK // 2, 2 * BLOCK), 1) < BLOCK
            for j in range(0, SUB, 2):
                one, two = x[j], x[j + 1]
                even = jnp.where(lower, one, halves_swapped(two))
                odd = jnp.where(lower, halves_swapped(one), two)
                pairs_ref[k * (part // 2) + g * (SUB // 2) + j // 2] = jnp.concatenate([even, odd], axis=0)
            return carry

        lax.fori_loop(0, part // SUB, body, 0)

    for k in range(LOADS // 2):
        arrange(k)
    for k in range(PIECES):
        locals_[k].wait()
        sends[k].wait_recv()

        def group(g, carry, k=k):
            sides = []
            for half in range(2):
                start = pl.multiple_of(k * piece + g * 2 * CELLS_AT_ONCE + half * CELLS_AT_ONCE, CELLS_AT_ONCE)
                sides.append(full[:, pl.ds(start, CELLS_AT_ONCE), :].reshape(slices * CELLS_AT_ONCE, ens))
            rhs = jnp.concatenate(sides, axis=1)
            out = jnp.dot(high, rhs, preferred_element_type=F32) + jnp.dot(low, rhs, preferred_element_type=F32)
            out = out.astype(BF16)
            for half in range(2):
                start = pl.multiple_of(k * piece + g * 2 * CELLS_AT_ONCE + half * CELLS_AT_ONCE, CELLS_AT_ONCE)
                panels_ref[:, pl.ds(start, CELLS_AT_ONCE), :] = out[:, half * ens : (half + 1) * ens].reshape(
                    slices, CELLS_AT_ONCE, ens
                )
            return carry

        lax.fori_loop(0, piece // (2 * CELLS_AT_ONCE), group, 0, unroll=2)
    for k in range(LOADS // 2, LOADS):
        arrange(k)
    for k in range(PIECES):
        sends[k].wait_send()


def both(one, two):
    zero = jnp.zeros_like(one)
    return jnp.concatenate(
        [jnp.concatenate([one, zero], axis=1), jnp.concatenate([zero, two], axis=1)], axis=0
    )


def products(index_ref, left_ref, right_ref, acc, to, source):
    acc[...] = jnp.zeros_like(acc)
    ens = acc.shape[2]

    def body(g, carry):
        for j in range(PAIRS):
            pair = g * PAIRS + j
            one = right_ref[index_ref[source, 2 * pair]]
            two = right_ref[index_ref[source, 2 * pair + 1]]
            out = jnp.dot(left_ref[pair], both(one, two), preferred_element_type=F32)
            acc[index_ref[to, 2 * pair]] += out[:, :ens]
            acc[index_ref[to, 2 * pair + 1]] += out[:, ens:]
        return carry

    lax.fori_loop(0, left_ref.shape[0] // PAIRS, body, 0)


def forward_kernel(index_ref, pairs_ref, panels_ref, part_ref, acc):
    products(index_ref, pairs_ref, panels_ref, acc, 0, 1)
    part_ref[...] = acc[pl.ds(0, part_ref.shape[0])].astype(BF16)


def exchange_kernel(
    regions, part_ref, obs_ref, inv_ref, pairs_ref, all_ref, own_ref, turned_ref, got, send_a, recv_a, send_b, recv_b
):
    me = lax.axis_index("region")
    rows, ens = obs_ref.shape
    barrier = pltpu.get_barrier_semaphore()
    for k in range(1, regions):
        peer = lax.rem(me + k, regions)
        pl.semaphore_signal(barrier, inc=1, device_id={"region": peer}, device_id_type=MESH)
    row = lax.broadcasted_iota(jnp.int32, (rows, rows), 0)
    col = lax.broadcasted_iota(jnp.int32, (rows, rows), 1)
    inner = row % BLOCK
    half = BLOCK // 2
    picked = (row // BLOCK) * BLOCK + (inner % half) * 2 + inner // half == col
    table = picked.astype(BF16)
    obs = jnp.dot(table, obs_ref[...], preferred_element_type=F32)
    inv = jnp.sum(jnp.where(picked, inv_ref[...], 0.0), axis=1, keepdims=True)
    pl.semaphore_wait(barrier, regions - 1)

    def first(k):
        peer = lax.rem(me + k, regions)
        return pltpu.make_async_remote_copy(
            src_ref=part_ref.at[peer],
            dst_ref=got.at[k],
            send_sem=send_a.at[k],
            recv_sem=recv_a.at[k],
            device_id={"region": peer},
            device_id_type=MESH,
        )

    def second(k):
        peer = lax.rem(me + k, regions)
        return pltpu.make_async_remote_copy(
            src_ref=all_ref.at[me],
            dst_ref=all_ref.at[me],
            send_sem=send_b.at[k],
            recv_sem=recv_b.at[k],
            device_id={"region": peer},
            device_id_type=MESH,
        )

    firsts = [first(k) for k in range(1, regions)]
    for copy in firsts:
        copy.start()

    pair_count = pairs_ref.shape[0]

    def turn(g, carry):
        for j in range(TURNS):
            x = pairs_ref[g * TURNS + j]
            stacked = jnp.concatenate([x, halves_swapped(x)], axis=0)
            turned_ref[g * TURNS + j] = stacked.T[:BLOCK]
        return carry

    lax.fori_loop(0, pair_count // TURNS // 2, turn, 0)
    evolved = part_ref[me].astype(F32)
    for k in range(1, regions):
        firsts[k - 1].wait_recv()
        evolved = evolved + got[k].astype(F32)
    misfit = (inv * (evolved - obs)).astype(BF16)
    all_ref[me] = misfit
    seconds = [second(k) for k in range(1, regions)]
    for copy in seconds:
        copy.start()
    own_ref[...] = lax.dot_general(
        table, misfit, (((0,), (0,)), ((), ())), preferred_element_type=F32
    ).astype(BF16)
    for copy in firsts:
        copy.wait_send()
    lax.fori_loop(pair_count // TURNS // 2, pair_count // TURNS, turn, 0)
    for k in range(1, regions):
        source = lax.rem(me - k + regions, regions)
        pltpu.make_async_remote_copy(
            src_ref=all_ref.at[source],
            dst_ref=all_ref.at[source],
            send_sem=send_b.at[k],
            recv_sem=recv_b.at[k],
            device_id={"region": source},
            device_id_type=MESH,
        ).wait_recv()
    for copy in seconds:
        copy.wait_send()


def adjoint_kernel(index_ref, turned_ref, misfit_ref, own_ref, acc, misfit_out):
    products(index_ref, turned_ref, misfit_ref, acc, 2, 3)
    misfit_out[...] = own_ref[...]


def gradient_kernel(acc_ref, blend_ref, mix_ref, grad_ref, mine, away, got, send_sem, recv_sem):
    me = lax.axis_index("window")
    other = 1 - me
    slabs, cells, ens = grad_ref.shape
    slices = 2 * slabs
    blocks = cells // BLOCK
    barrier = pltpu.get_barrier_semaphore()
    pl.semaphore_signal(barrier, inc=1, device_id={"window": other}, device_id_type=MESH)
    high, low = spread(blend_ref[...], CELLS_AT_ONCE)
    mix = mix_ref[...]
    pl.semaphore_wait(barrier, 1)

    def send(block):
        return pltpu.make_async_remote_copy(
            src_ref=away.at[block],
            dst_ref=got.at[block],
            send_sem=send_sem.at[block],
            recv_sem=recv_sem.at[block],
            device_id={"window": other},
            device_id_type=MESH,
        )

    def pull(block):
        for within in range(BLOCK // (2 * CELLS_AT_ONCE)):
            sides = []
            for half in range(2):
                start = (2 * within + half) * CELLS_AT_ONCE
                rows = [acc_ref[t * blocks + block, pl.ds(start, CELLS_AT_ONCE), :] for t in range(slices)]
                sides.append(jnp.concatenate(rows, axis=0))
            rhs = jnp.concatenate(sides, axis=1)
            rhs_high = rhs.astype(BF16)
            rhs_low = (rhs - rhs_high.astype(F32)).astype(BF16)
            dims = (((0,), (0,)), ((), ()))
            out = lax.dot_general(high, rhs_high, dims, preferred_element_type=F32)
            out = out + lax.dot_general(low, rhs_high, dims, preferred_element_type=F32)
            out = (out + lax.dot_general(high, rhs_low, dims, preferred_element_type=F32)).astype(BF16)
            for half in range(2):
                start = (2 * within + half) * CELLS_AT_ONCE
                piece = out[:, half * ens : (half + 1) * ens].reshape(slices, CELLS_AT_ONCE, ens)
                first, second = piece[:slabs], piece[slabs:]
                mine[block, :, pl.ds(start, CELLS_AT_ONCE), :] = jnp.where(me == 0, first, second)
                away[block, :, pl.ds(start, CELLS_AT_ONCE), :] = jnp.where(me == 0, second, first)

    def finish(block):
        send(block).wait_recv()
        total = (mine[block].astype(F32) + got[block].astype(F32)).astype(BF16).reshape(slabs * BLOCK, ens)
        grad = jnp.dot(total, mix, preferred_element_type=F32).astype(BF16)
        grad_ref[:, pl.ds(block * BLOCK, BLOCK), :] = grad.reshape(slabs, BLOCK, ens)

    for block in range(blocks):
        pull(block)
        send(block).start()
        if block >= LAG:
            finish(block - LAG)
    for block in range(blocks - LAG, blocks):
        finish(block)
    for block in range(blocks):
        send(block).wait_send()


def vmem():
    return pl.BlockSpec(memory_space=pltpu.VMEM)


def shards(
    regions,
    flux,
    blend,
    footprints,
    receptor_block,
    cell_block,
    slice_index,
    live_counts,
    observed,
    inv_var,
    prior_mix,
):
    slabs, cells, ens = flux.shape
    slices = blend.shape[0]
    cell_blocks = cells // BLOCK
    panel_total = slices * cell_blocks
    slots = footprints.shape[1]
    rows = observed.shape[1]
    own_blocks = rows // BLOCK
    window_blocks = own_blocks * regions

    panels, pairs, index = pl.pallas_call(
        functools.partial(blend_kernel, window_blocks),
        out_shape=(
            jax.ShapeDtypeStruct((slices, cells, ens), BF16),
            jax.ShapeDtypeStruct((slots // 2, BLOCK, 2 * BLOCK), BF16),
            jax.ShapeDtypeStruct((4, slots), jnp.int32),
        ),
        in_specs=[vmem()] * 4 + [pl.BlockSpec(memory_space=pltpu.HBM)] * 3,
        out_specs=(vmem(), vmem(), vmem()),
        scratch_shapes=[
            pltpu.VMEM((slices, cells, ens), BF16),
            pltpu.VMEM((slots, BLOCK * BLOCK), BF16),
            pltpu.VMEM((slices, slices), F32),
            pltpu.SemaphoreType.DMA,
            pltpu.SemaphoreType.DMA((LOADS,)),
            pltpu.SemaphoreType.DMA((PIECES,)),
            pltpu.SemaphoreType.DMA((PIECES,)),
            pltpu.SemaphoreType.DMA((PIECES,)),
        ],
        compiler_params=pltpu.CompilerParams(collective_id=0, has_side_effects=True, vmem_limit_bytes=32 << 20),
        name="blend_slices",
    )(receptor_block, cell_block, slice_index, live_counts, blend, flux, footprints)

    smem = pl.BlockSpec(memory_space=pltpu.SMEM)
    part = pl.pallas_call(
        forward_kernel,
        out_shape=jax.ShapeDtypeStruct((window_blocks, BLOCK, ens), BF16),
        in_specs=[smem, vmem(), vmem()],
        out_specs=vmem(),
        scratch_shapes=[pltpu.VMEM((window_blocks + 1, BLOCK, ens), F32)],
        compiler_params=pltpu.CompilerParams(vmem_limit_bytes=32 << 20),
        name="forward_blocks",
    )(index, pairs, panels.reshape(panel_total, BLOCK, ens))

    misfit_all, own, turned = pl.pallas_call(
        functools.partial(exchange_kernel, regions),
        out_shape=(
            jax.ShapeDtypeStruct((regions, rows, ens), BF16),
            jax.ShapeDtypeStruct((rows, ens), BF16),
            jax.ShapeDtypeStruct((slots // 2, BLOCK, 2 * BLOCK), BF16),
        ),
        in_specs=[vmem()] * 4,
        out_specs=(vmem(), vmem(), vmem()),
        scratch_shapes=[
            pltpu.VMEM((regions, rows, ens), BF16),
            pltpu.SemaphoreType.DMA((regions,)),
            pltpu.SemaphoreType.DMA((regions,)),
            pltpu.SemaphoreType.DMA((regions,)),
            pltpu.SemaphoreType.DMA((regions,)),
        ],
        compiler_params=pltpu.CompilerParams(collective_id=1, has_side_effects=True, vmem_limit_bytes=32 << 20),
        name="misfit_exchange",
    )(part.reshape(regions, rows, ens), observed[0], inv_var, pairs)

    collected, misfit = pl.pallas_call(
        adjoint_kernel,
        out_shape=(
            jax.ShapeDtypeStruct((panel_total + 1, BLOCK, ens), F32),
            jax.ShapeDtypeStruct((rows, ens), BF16),
        ),
        in_specs=[smem, vmem(), vmem(), vmem()],
        out_specs=(vmem(), vmem()),
        compiler_params=pltpu.CompilerParams(vmem_limit_bytes=32 << 20),
        name="adjoint_blocks",
    )(index, turned, misfit_all.reshape(window_blocks, BLOCK, ens), own)

    blocks_shape = (cell_blocks, slabs, BLOCK, ens)
    gradient = pl.pallas_call(
        gradient_kernel,
        out_shape=jax.ShapeDtypeStruct((slabs, cells, ens), BF16),
        in_specs=[vmem(), vmem(), vmem()],
        out_specs=vmem(),
        scratch_shapes=[
            pltpu.VMEM(blocks_shape, BF16),
            pltpu.VMEM(blocks_shape, BF16),
            pltpu.VMEM(blocks_shape, BF16),
            pltpu.SemaphoreType.DMA((cell_blocks,)),
            pltpu.SemaphoreType.DMA((cell_blocks,)),
        ],
        compiler_params=pltpu.CompilerParams(collective_id=2, has_side_effects=True, vmem_limit_bytes=32 << 20),
        name="gradient_exchange",
    )(collected, blend, prior_mix)
    return misfit[None], gradient


def solution(mesh):
    in_specs = (
        P(("group", "window"), "region", None),
        P(),
        P(("group", "window"), "region", None),
        P(("group", "window"), "region"),
        P(("group", "window"), "region"),
        P(("group", "window"), "region"),
        P(("group", "window"), "region"),
        P(("group", "window"), "region", None),
        P(("group", "window"), "region"),
        P(),
    )
    out_specs = (P(("group", "window"), "region", None), P(("group", "window"), "region", None))
    return jax.shard_map(
        functools.partial(shards, mesh.shape["region"]),
        mesh=mesh,
        in_specs=in_specs,
        out_specs=out_specs,
        check_vma=False,
    )
```

```python
import functools

import jax
import jax.numpy as jnp
from jax import lax
from jax.experimental import pallas as pl
from jax.experimental.pallas import tpu as pltpu
from jax.sharding import PartitionSpec as P

BLOCK = 64
MESH = pl.DeviceIdType.MESH
F32 = jnp.float32
BF16 = jnp.bfloat16
SUB = 16
SUBS = 4
CELLS_AT_ONCE = 16
PIECES = 4
LOADS = 8
PAIRS = 32
TURNS = 32
LAG = 2


def spread(matrix, width):
    size = matrix.shape[0]
    full = size * width
    row = lax.broadcasted_iota(jnp.int32, (full, size), 0)
    col = lax.broadcasted_iota(jnp.int32, (full, size), 1)
    pick = (row // width == col).astype(BF16)
    row_f = lax.broadcasted_iota(jnp.int32, (full, full), 0)
    col_f = lax.broadcasted_iota(jnp.int32, (full, full), 1)
    same = row_f % width == col_f % width
    high = matrix.astype(BF16)
    low = (matrix - high.astype(F32)).astype(BF16)
    parts = []
    for part in (high, low):
        tall = jnp.dot(pick, part, preferred_element_type=F32).astype(BF16)
        wide = lax.dot_general(tall, pick, (((1,), (1,)), ((), ())), preferred_element_type=F32)
        parts.append(jnp.where(same, wide, 0.0).astype(BF16))
    return parts


def halves_swapped(x):
    return pltpu.roll(x, BLOCK, 1)


def blend_kernel(
    window_blocks,
    recv_hbm,
    cell_hbm,
    slice_hbm,
    live_ref,
    blend_hbm,
    flux_hbm,
    fp_hbm,
    panels_ref,
    pairs_ref,
    index_ref,
    full,
    raw,
    blend_ref,
    recv_ref,
    cell_ref,
    slice_ref,
    small_sem,
    fp_sem,
    local_sem,
    send_sem,
    recv_sem,
):
    me = lax.axis_index("window")
    other = 1 - me
    slabs, cells, ens = flux_hbm.shape
    slices = panels_ref.shape[0]
    slots = raw.shape[0]
    barrier = pltpu.get_barrier_semaphore()
    pl.semaphore_signal(barrier, inc=1, device_id={"window": other}, device_id_type=MESH)
    smalls = [
        pltpu.make_async_copy(source, target, small_sem.at[k])
        for k, (source, target) in enumerate(
            ((blend_hbm, blend_ref), (recv_hbm, recv_ref), (cell_hbm, cell_ref), (slice_hbm, slice_ref))
        )
    ]
    for copy in smalls:
        copy.start()
    piece = cells // PIECES
    locals_, sends, loads = [], [], []
    for k in range(PIECES):
        span = pl.ds(k * piece, piece)
        locals_.append(
            pltpu.make_async_copy(
                flux_hbm.at[:, span, :], full.at[pl.ds(me * slabs, slabs), span, :], local_sem.at[k]
            )
        )
        locals_[-1].start()
    part = slots // LOADS
    for k in range(LOADS):
        span = pl.ds(k * part, part)
        loads.append(pltpu.make_async_copy(fp_hbm.at[0, span, :], raw.at[span, :], fp_sem.at[k]))
    loads[0].start()
    pl.semaphore_wait(barrier, 1)
    for k in range(PIECES):
        span = pl.ds(k * piece, piece)
        sends.append(
            pltpu.make_async_remote_copy(
                src_ref=flux_hbm.at[:, span, :],
                dst_ref=full.at[pl.ds(me * slabs, slabs), span, :],
                send_sem=send_sem.at[k],
                recv_sem=recv_sem.at[k],
                device_id={"window": other},
                device_id_type=MESH,
            )
        )
        sends[-1].start()
    for k in range(1, LOADS):
        loads[k].start()

    for copy in smalls:
        copy.wait()
    cell_blocks = cells // BLOCK
    live = lax.broadcasted_iota(jnp.int32, recv_ref.shape, 1) < live_ref[...]
    panel = slice_ref[...] * cell_blocks + cell_ref[...]
    index_ref[pl.ds(0, 1), :] = jnp.where(live, recv_ref[...], window_blocks)
    index_ref[pl.ds(1, 1), :] = jnp.where(live, panel, 0)
    index_ref[pl.ds(2, 1), :] = jnp.where(live, panel, slices * cell_blocks)
    index_ref[pl.ds(3, 1), :] = jnp.where(live, recv_ref[...], 0)
    high, low = spread(blend_ref[...], CELLS_AT_ONCE)

    def arrange(k):
        loads[k].wait()

        def body(g, carry):
            lower = lax.broadcasted_iota(jnp.int32, (BLOCK // 2, 2 * BLOCK), 1) < BLOCK
            for sub in range(SUBS):
                base = pl.multiple_of(k * part + g * SUBS * SUB + sub * SUB, SUB)
                x = raw[pl.ds(base, SUB), :].reshape(SUB, BLOCK // 2, 2 * BLOCK)
                for j in range(0, SUB, 2):
                    one, two = x[j], x[j + 1]
                    even = jnp.where(lower, one, halves_swapped(two))
                    odd = jnp.where(lower, halves_swapped(one), two)
                    place = k * (part // 2) + (g * SUBS + sub) * (SUB // 2) + j // 2
                    pairs_ref[place] = jnp.concatenate([even, odd], axis=0)
            return carry

        lax.fori_loop(0, part // SUB // SUBS, body, 0)

    for k in range(LOADS // 2):
        arrange(k)
    for k in range(PIECES):
        locals_[k].wait()
        sends[k].wait_recv()

        def group(g, carry, k=k):
            sides = []
            for half in range(2):
                start = pl.multiple_of(k * piece + g * 2 * CELLS_AT_ONCE + half * CELLS_AT_ONCE, CELLS_AT_ONCE)
                sides.append(full[:, pl.ds(start, CELLS_AT_ONCE), :].reshape(slices * CELLS_AT_ONCE, ens))
            rhs = jnp.concatenate(sides, axis=1)
            out = jnp.dot(high, rhs, preferred_element_type=F32) + jnp.dot(low, rhs, preferred_element_type=F32)
            out = out.astype(BF16)
            for half in range(2):
                start = pl.multiple_of(k * piece + g * 2 * CELLS_AT_ONCE + half * CELLS_AT_ONCE, CELLS_AT_ONCE)
                panels_ref[:, pl.ds(start, CELLS_AT_ONCE), :] = out[:, half * ens : (half + 1) * ens].reshape(
                    slices, CELLS_AT_ONCE, ens
                )
            return carry

        lax.fori_loop(0, piece // (2 * CELLS_AT_ONCE), group, 0, unroll=2)
    for k in range(LOADS // 2, LOADS):
        arrange(k)
    for k in range(PIECES):
        sends[k].wait_send()


def both(one, two):
    zero = jnp.zeros_like(one)
    return jnp.concatenate(
        [jnp.concatenate([one, zero], axis=1), jnp.concatenate([zero, two], axis=1)], axis=0
    )


def products(index_ref, left_ref, right_ref, acc, to, source):
    acc[...] = jnp.zeros_like(acc)
    ens = acc.shape[2]

    def body(g, carry):
        for j in range(PAIRS):
            pair = g * PAIRS + j
            one = right_ref[index_ref[source, 2 * pair]]
            two = right_ref[index_ref[source, 2 * pair + 1]]
            out = jnp.dot(left_ref[pair], both(one, two), preferred_element_type=F32)
            acc[index_ref[to, 2 * pair]] += out[:, :ens]
            acc[index_ref[to, 2 * pair + 1]] += out[:, ens:]
        return carry

    lax.fori_loop(0, left_ref.shape[0] // PAIRS, body, 0)


def forward_kernel(index_ref, pairs_ref, panels_ref, part_ref, acc):
    products(index_ref, pairs_ref, panels_ref, acc, 0, 1)
    part_ref[...] = acc[pl.ds(0, part_ref.shape[0])].astype(BF16)


def exchange_kernel(
    regions, part_ref, obs_ref, inv_ref, pairs_ref, all_ref, own_ref, turned_ref, got, send_a, recv_a, send_b, recv_b
):
    me = lax.axis_index("region")
    rows, ens = obs_ref.shape
    barrier = pltpu.get_barrier_semaphore()
    for k in range(1, regions):
        peer = lax.rem(me + k, regions)
        pl.semaphore_signal(barrier, inc=1, device_id={"region": peer}, device_id_type=MESH)
    row = lax.broadcasted_iota(jnp.int32, (rows, rows), 0)
    col = lax.broadcasted_iota(jnp.int32, (rows, rows), 1)
    inner = row % BLOCK
    half = BLOCK // 2
    picked = (row // BLOCK) * BLOCK + (inner % half) * 2 + inner // half == col
    table = picked.astype(BF16)
    obs = jnp.dot(table, obs_ref[...], preferred_element_type=F32)
    inv = jnp.sum(jnp.where(picked, inv_ref[...], 0.0), axis=1, keepdims=True)
    pl.semaphore_wait(barrier, regions - 1)

    def first(k):
        peer = lax.rem(me + k, regions)
        return pltpu.make_async_remote_copy(
            src_ref=part_ref.at[peer],
            dst_ref=got.at[k],
            send_sem=send_a.at[k],
            recv_sem=recv_a.at[k],
            device_id={"region": peer},
            device_id_type=MESH,
        )

    def second(k):
        peer = lax.rem(me + k, regions)
        return pltpu.make_async_remote_copy(
            src_ref=all_ref.at[me],
            dst_ref=all_ref.at[me],
            send_sem=send_b.at[k],
            recv_sem=recv_b.at[k],
            device_id={"region": peer},
            device_id_type=MESH,
        )

    firsts = [first(k) for k in range(1, regions)]
    for copy in firsts:
        copy.start()

    pair_count = pairs_ref.shape[0]

    def turn(g, carry):
        for j in range(TURNS):
            x = pairs_ref[g * TURNS + j]
            stacked = jnp.concatenate([x, halves_swapped(x)], axis=0)
            turned_ref[g * TURNS + j] = stacked.T[:BLOCK]
        return carry

    lax.fori_loop(0, pair_count // TURNS // 2, turn, 0)
    evolved = part_ref[me].astype(F32)
    for k in range(1, regions):
        firsts[k - 1].wait_recv()
        evolved = evolved + got[k].astype(F32)
    misfit = (inv * (evolved - obs)).astype(BF16)
    all_ref[me] = misfit
    seconds = [second(k) for k in range(1, regions)]
    for copy in seconds:
        copy.start()
    own_ref[...] = lax.dot_general(
        table, misfit, (((0,), (0,)), ((), ())), preferred_element_type=F32
    ).astype(BF16)
    for copy in firsts:
        copy.wait_send()
    lax.fori_loop(pair_count // TURNS // 2, pair_count // TURNS, turn, 0)
    for k in range(1, regions):
        source = lax.rem(me - k + regions, regions)
        pltpu.make_async_remote_copy(
            src_ref=all_ref.at[source],
            dst_ref=all_ref.at[source],
            send_sem=send_b.at[k],
            recv_sem=recv_b.at[k],
            device_id={"region": source},
            device_id_type=MESH,
        ).wait_recv()
    for copy in seconds:
        copy.wait_send()


def adjoint_kernel(index_ref, turned_ref, misfit_ref, own_ref, acc, misfit_out):
    products(index_ref, turned_ref, misfit_ref, acc, 2, 3)
    misfit_out[...] = own_ref[...]


def gradient_kernel(acc_ref, blend_ref, mix_ref, grad_ref, mine, away, got, send_sem, recv_sem):
    me = lax.axis_index("window")
    other = 1 - me
    slabs, cells, ens = grad_ref.shape
    slices = 2 * slabs
    blocks = cells // BLOCK
    barrier = pltpu.get_barrier_semaphore()
    pl.semaphore_signal(barrier, inc=1, device_id={"window": other}, device_id_type=MESH)
    high, low = spread(blend_ref[...], CELLS_AT_ONCE)
    mix = mix_ref[...]
    pl.semaphore_wait(barrier, 1)

    def send(block):
        return pltpu.make_async_remote_copy(
            src_ref=away.at[block],
            dst_ref=got.at[block],
            send_sem=send_sem.at[block],
            recv_sem=recv_sem.at[block],
            device_id={"window": other},
            device_id_type=MESH,
        )

    def pull(block):
        for within in range(BLOCK // (2 * CELLS_AT_ONCE)):
            sides = []
            for half in range(2):
                start = (2 * within + half) * CELLS_AT_ONCE
                rows = [acc_ref[t * blocks + block, pl.ds(start, CELLS_AT_ONCE), :] for t in range(slices)]
                sides.append(jnp.concatenate(rows, axis=0))
            rhs = jnp.concatenate(sides, axis=1)
            rhs_high = rhs.astype(BF16)
            rhs_low = (rhs - rhs_high.astype(F32)).astype(BF16)
            dims = (((0,), (0,)), ((), ()))
            out = lax.dot_general(high, rhs_high, dims, preferred_element_type=F32)
            out = out + lax.dot_general(low, rhs_high, dims, preferred_element_type=F32)
            out = (out + lax.dot_general(high, rhs_low, dims, preferred_element_type=F32)).astype(BF16)
            for half in range(2):
                start = (2 * within + half) * CELLS_AT_ONCE
                piece = out[:, half * ens : (half + 1) * ens].reshape(slices, CELLS_AT_ONCE, ens)
                first, second = piece[:slabs], piece[slabs:]
                mine[block, :, pl.ds(start, CELLS_AT_ONCE), :] = jnp.where(me == 0, first, second)
                away[block, :, pl.ds(start, CELLS_AT_ONCE), :] = jnp.where(me == 0, second, first)

    def finish(block):
        send(block).wait_recv()
        total = (mine[block].astype(F32) + got[block].astype(F32)).astype(BF16).reshape(slabs * BLOCK, ens)
        grad = jnp.dot(total, mix, preferred_element_type=F32).astype(BF16)
        grad_ref[:, pl.ds(block * BLOCK, BLOCK), :] = grad.reshape(slabs, BLOCK, ens)

    for block in range(blocks):
        pull(block)
        send(block).start()
        if block >= LAG:
            finish(block - LAG)
    for block in range(blocks - LAG, blocks):
        finish(block)
    for block in range(blocks):
        send(block).wait_send()


def vmem():
    return pl.BlockSpec(memory_space=pltpu.VMEM)


def hbm():
    return pl.BlockSpec(memory_space=pltpu.HBM)


def stay(x):
    return pltpu.with_memory_space_constraint(x, pltpu.HBM)


def shards(
    regions,
    flux,
    blend,
    footprints,
    receptor_block,
    cell_block,
    slice_index,
    live_counts,
    observed,
    inv_var,
    prior_mix,
):
    slabs, cells, ens = flux.shape
    slices = blend.shape[0]
    cell_blocks = cells // BLOCK
    panel_total = slices * cell_blocks
    slots = footprints.shape[1]
    rows = observed.shape[1]
    own_blocks = rows // BLOCK
    window_blocks = own_blocks * regions

    panels, pairs, index = pl.pallas_call(
        functools.partial(blend_kernel, window_blocks),
        out_shape=(
            jax.ShapeDtypeStruct((slices, cells, ens), BF16),
            jax.ShapeDtypeStruct((slots // 2, BLOCK, 2 * BLOCK), BF16),
            jax.ShapeDtypeStruct((4, slots), jnp.int32),
        ),
        in_specs=[hbm()] * 3 + [vmem()] + [hbm()] * 3,
        out_specs=(vmem(), vmem(), vmem()),
        scratch_shapes=[
            pltpu.VMEM((slices, cells, ens), BF16),
            pltpu.VMEM((slots, BLOCK * BLOCK), BF16),
            pltpu.VMEM((slices, slices), F32),
            pltpu.VMEM((1, slots), jnp.int32),
            pltpu.VMEM((1, slots), jnp.int32),
            pltpu.VMEM((1, slots), jnp.int32),
            pltpu.SemaphoreType.DMA((4,)),
            pltpu.SemaphoreType.DMA((LOADS,)),
            pltpu.SemaphoreType.DMA((PIECES,)),
            pltpu.SemaphoreType.DMA((PIECES,)),
            pltpu.SemaphoreType.DMA((PIECES,)),
        ],
        compiler_params=pltpu.CompilerParams(collective_id=0, has_side_effects=True, vmem_limit_bytes=24 << 20),
        name="blend_slices",
    )(
        stay(receptor_block),
        stay(cell_block),
        stay(slice_index),
        live_counts,
        stay(blend),
        stay(flux),
        stay(footprints),
    )

    smem = pl.BlockSpec(memory_space=pltpu.SMEM)
    part = pl.pallas_call(
        forward_kernel,
        out_shape=jax.ShapeDtypeStruct((window_blocks, BLOCK, ens), BF16),
        in_specs=[smem, vmem(), vmem()],
        out_specs=vmem(),
        scratch_shapes=[pltpu.VMEM((window_blocks + 1, BLOCK, ens), F32)],
        compiler_params=pltpu.CompilerParams(vmem_limit_bytes=16 << 20),
        name="forward_blocks",
    )(index, pairs, panels.reshape(panel_total, BLOCK, ens))

    misfit_all, own, turned = pl.pallas_call(
        functools.partial(exchange_kernel, regions),
        out_shape=(
            jax.ShapeDtypeStruct((regions, rows, ens), BF16),
            jax.ShapeDtypeStruct((rows, ens), BF16),
            jax.ShapeDtypeStruct((slots // 2, BLOCK, 2 * BLOCK), BF16),
        ),
        in_specs=[vmem()] * 4,
        out_specs=(vmem(), vmem(), vmem()),
        scratch_shapes=[
            pltpu.VMEM((regions, rows, ens), BF16),
            pltpu.SemaphoreType.DMA((regions,)),
            pltpu.SemaphoreType.DMA((regions,)),
            pltpu.SemaphoreType.DMA((regions,)),
            pltpu.SemaphoreType.DMA((regions,)),
        ],
        compiler_params=pltpu.CompilerParams(collective_id=1, has_side_effects=True, vmem_limit_bytes=16 << 20),
        name="misfit_exchange",
    )(part.reshape(regions, rows, ens), observed[0], inv_var, pairs)

    collected, misfit = pl.pallas_call(
        adjoint_kernel,
        out_shape=(
            jax.ShapeDtypeStruct((panel_total + 1, BLOCK, ens), F32),
            jax.ShapeDtypeStruct((rows, ens), BF16),
        ),
        in_specs=[smem, vmem(), vmem(), vmem()],
        out_specs=(vmem(), vmem()),
        compiler_params=pltpu.CompilerParams(vmem_limit_bytes=16 << 20),
        name="adjoint_blocks",
    )(index, turned, misfit_all.reshape(window_blocks, BLOCK, ens), own)

    blocks_shape = (cell_blocks, slabs, BLOCK, ens)
    gradient = pl.pallas_call(
        gradient_kernel,
        out_shape=jax.ShapeDtypeStruct((slabs, cells, ens), BF16),
        in_specs=[vmem(), vmem(), vmem()],
        out_specs=vmem(),
        scratch_shapes=[
            pltpu.VMEM(blocks_shape, BF16),
            pltpu.VMEM(blocks_shape, BF16),
            pltpu.VMEM(blocks_shape, BF16),
            pltpu.SemaphoreType.DMA((cell_blocks,)),
            pltpu.SemaphoreType.DMA((cell_blocks,)),
        ],
        compiler_params=pltpu.CompilerParams(collective_id=2, has_side_effects=True, vmem_limit_bytes=16 << 20),
        name="gradient_exchange",
    )(collected, blend, prior_mix)
    return misfit[None], gradient


def solution(mesh):
    in_specs = (
        P(("group", "window"), "region", None),
        P(),
        P(("group", "window"), "region", None),
        P(("group", "window"), "region"),
        P(("group", "window"), "region"),
        P(("group", "window"), "region"),
        P(("group", "window"), "region"),
        P(("group", "window"), "region", None),
        P(("group", "window"), "region"),
        P(),
    )
    out_specs = (P(("group", "window"), "region", None), P(("group", "window"), "region", None))
    return jax.shard_map(
        functools.partial(shards, mesh.shape["region"]),
        mesh=mesh,
        in_specs=in_specs,
        out_specs=out_specs,
        check_vma=False,
    )
```

```python
import functools

import jax
import jax.numpy as jnp
from jax import lax
from jax.experimental import pallas as pl
from jax.experimental.pallas import tpu as pltpu
from jax.sharding import PartitionSpec as P

BLOCK = 64
MESH = pl.DeviceIdType.MESH
F32 = jnp.float32
BF16 = jnp.bfloat16
SUB = 16
SUBS = 4
CELLS_AT_ONCE = 16
PIECES = 4
LOADS = 8
PAIRS = 32
TURNS = 32
LAG = 2


def spread(matrix, width):
    size = matrix.shape[0]
    full = size * width
    row = lax.broadcasted_iota(jnp.int32, (full, size), 0)
    col = lax.broadcasted_iota(jnp.int32, (full, size), 1)
    pick = (row // width == col).astype(BF16)
    row_f = lax.broadcasted_iota(jnp.int32, (full, full), 0)
    col_f = lax.broadcasted_iota(jnp.int32, (full, full), 1)
    same = row_f % width == col_f % width
    high = matrix.astype(BF16)
    low = (matrix - high.astype(F32)).astype(BF16)
    parts = []
    for part in (high, low):
        tall = jnp.dot(pick, part, preferred_element_type=F32).astype(BF16)
        wide = lax.dot_general(tall, pick, (((1,), (1,)), ((), ())), preferred_element_type=F32)
        parts.append(jnp.where(same, wide, 0.0).astype(BF16))
    return parts


def halves_swapped(x):
    return pltpu.roll(x, BLOCK, 1)


def blend_kernel(
    window_blocks,
    recv_hbm,
    cell_hbm,
    slice_hbm,
    live_ref,
    blend_hbm,
    flux_hbm,
    fp_hbm,
    panels_ref,
    raw,
    index_ref,
    full,
    blend_ref,
    recv_ref,
    cell_ref,
    slice_ref,
    small_sem,
    fp_sem,
    local_sem,
    send_sem,
    recv_sem,
):
    me = lax.axis_index("window")
    other = 1 - me
    slabs, cells, ens = flux_hbm.shape
    slices = panels_ref.shape[0]
    slots = raw.shape[0]
    barrier = pltpu.get_barrier_semaphore()
    pl.semaphore_signal(barrier, inc=1, device_id={"window": other}, device_id_type=MESH)
    smalls = [
        pltpu.make_async_copy(source, target, small_sem.at[k])
        for k, (source, target) in enumerate(
            ((blend_hbm, blend_ref), (recv_hbm, recv_ref), (cell_hbm, cell_ref), (slice_hbm, slice_ref))
        )
    ]
    for copy in smalls:
        copy.start()
    piece = cells // PIECES
    locals_, sends, loads = [], [], []
    for k in range(PIECES):
        span = pl.ds(k * piece, piece)
        locals_.append(
            pltpu.make_async_copy(
                flux_hbm.at[:, span, :], full.at[pl.ds(me * slabs, slabs), span, :], local_sem.at[k]
            )
        )
        locals_[-1].start()
    part = slots // LOADS
    for k in range(LOADS):
        span = pl.ds(k * part, part)
        loads.append(pltpu.make_async_copy(fp_hbm.at[0, span, :], raw.at[span, :], fp_sem.at[k]))
    loads[0].start()
    pl.semaphore_wait(barrier, 1)
    for k in range(PIECES):
        span = pl.ds(k * piece, piece)
        sends.append(
            pltpu.make_async_remote_copy(
                src_ref=flux_hbm.at[:, span, :],
                dst_ref=full.at[pl.ds(me * slabs, slabs), span, :],
                send_sem=send_sem.at[k],
                recv_sem=recv_sem.at[k],
                device_id={"window": other},
                device_id_type=MESH,
            )
        )
        sends[-1].start()
    for k in range(1, LOADS):
        loads[k].start()

    for copy in smalls:
        copy.wait()
    cell_blocks = cells // BLOCK
    live = lax.broadcasted_iota(jnp.int32, recv_ref.shape, 1) < live_ref[...]
    panel = slice_ref[...] * cell_blocks + cell_ref[...]
    index_ref[pl.ds(0, 1), :] = jnp.where(live, recv_ref[...], window_blocks)
    index_ref[pl.ds(1, 1), :] = jnp.where(live, panel, 0)
    index_ref[pl.ds(2, 1), :] = jnp.where(live, panel, slices * cell_blocks)
    index_ref[pl.ds(3, 1), :] = jnp.where(live, recv_ref[...], 0)
    high, low = spread(blend_ref[...], CELLS_AT_ONCE)

    for k in range(PIECES):
        locals_[k].wait()
        sends[k].wait_recv()

        def group(g, carry, k=k):
            sides = []
            for half in range(2):
                start = pl.multiple_of(k * piece + g * 2 * CELLS_AT_ONCE + half * CELLS_AT_ONCE, CELLS_AT_ONCE)
                sides.append(full[:, pl.ds(start, CELLS_AT_ONCE), :].reshape(slices * CELLS_AT_ONCE, ens))
            rhs = jnp.concatenate(sides, axis=1)
            out = jnp.dot(high, rhs, preferred_element_type=F32) + jnp.dot(low, rhs, preferred_element_type=F32)
            out = out.astype(BF16)
            for half in range(2):
                start = pl.multiple_of(k * piece + g * 2 * CELLS_AT_ONCE + half * CELLS_AT_ONCE, CELLS_AT_ONCE)
                panels_ref[:, pl.ds(start, CELLS_AT_ONCE), :] = out[:, half * ens : (half + 1) * ens].reshape(
                    slices, CELLS_AT_ONCE, ens
                )
            return carry

        lax.fori_loop(0, piece // (2 * CELLS_AT_ONCE), group, 0, unroll=2)
    for k in range(PIECES):
        sends[k].wait_send()
    for copy in loads:
        copy.wait()


def both(one, two):
    zero = jnp.zeros_like(one)
    return jnp.concatenate(
        [jnp.concatenate([one, zero], axis=1), jnp.concatenate([zero, two], axis=1)], axis=0
    )


def turned_pair(x):
    t = x.T
    return jnp.concatenate([t[:BLOCK], t[BLOCK:]], axis=1)


def add_products(index_ref, left, right_ref, acc, to, source, pair):
    ens = acc.shape[2]
    one = right_ref[index_ref[source, 2 * pair]]
    two = right_ref[index_ref[source, 2 * pair + 1]]
    out = jnp.dot(left, both(one, two), preferred_element_type=F32)
    acc[index_ref[to, 2 * pair]] += out[:, :ens]
    acc[index_ref[to, 2 * pair + 1]] += out[:, ens:]


def forward_kernel(index_ref, raw, panels_ref, part_ref, turned_ref, pairs_ref, acc):
    acc[...] = jnp.zeros_like(acc)
    early = turned_ref.shape[0]

    def body(turning, g, carry):
        lower = lax.broadcasted_iota(jnp.int32, (BLOCK // 2, 2 * BLOCK), 1) < BLOCK
        for sub in range(SUBS):
            group = g * SUBS + sub
            base = pl.multiple_of(group * SUB, SUB)
            x = raw[pl.ds(base, SUB), :].reshape(SUB, BLOCK // 2, 2 * BLOCK)
            for j in range(0, SUB, 2):
                one, two = x[j], x[j + 1]
                even = jnp.where(lower, one, halves_swapped(two))
                odd = jnp.where(lower, halves_swapped(one), two)
                left = jnp.concatenate([even, odd], axis=0)
                pair = group * (SUB // 2) + j // 2
                if turning:
                    turned_ref[pair] = turned_pair(left)
                else:
                    pairs_ref[pair - early] = left
                add_products(index_ref, left, panels_ref, acc, 0, 1, pair)
        return carry

    each = SUBS * SUB // 2
    lax.fori_loop(0, early // each, functools.partial(body, True), 0)
    lax.fori_loop(early // each, raw.shape[0] // (2 * each), functools.partial(body, False), 0)
    part_ref[...] = acc[pl.ds(0, part_ref.shape[0])].astype(BF16)


def exchange_kernel(
    regions, part_ref, obs_ref, inv_ref, pairs_ref, all_ref, own_ref, turned_ref, got, send_a, recv_a, send_b, recv_b, send_c, recv_c
):
    me = lax.axis_index("region")
    rows, ens = obs_ref.shape
    barrier = pltpu.get_barrier_semaphore()
    for k in range(1, regions):
        peer = lax.rem(me + k, regions)
        pl.semaphore_signal(barrier, inc=1, device_id={"region": peer}, device_id_type=MESH)
    row = lax.broadcasted_iota(jnp.int32, (rows, rows), 0)
    col = lax.broadcasted_iota(jnp.int32, (rows, rows), 1)
    inner = row % BLOCK
    half = BLOCK // 2
    picked = (row // BLOCK) * BLOCK + (inner % half) * 2 + inner // half == col
    table = picked.astype(BF16)
    obs = jnp.dot(table, obs_ref[...], preferred_element_type=F32)
    inv = jnp.sum(jnp.where(picked, inv_ref[...], 0.0), axis=1, keepdims=True)
    pl.semaphore_wait(barrier, regions - 1)

    def first(k):
        peer = lax.rem(me + k, regions)
        return pltpu.make_async_remote_copy(
            src_ref=part_ref.at[peer],
            dst_ref=got.at[k],
            send_sem=send_a.at[k],
            recv_sem=recv_a.at[k],
            device_id={"region": peer},
            device_id_type=MESH,
        )

    width = 2 if regions % 2 == 0 else 1
    count = regions // width
    high, low = me // width, lax.rem(me, width)

    def at(k, low):
        return lax.rem(high + count - k, count) * width + low

    def along(k, source):
        return pltpu.make_async_remote_copy(
            src_ref=all_ref.at[source],
            dst_ref=all_ref.at[source],
            send_sem=send_b.at[k],
            recv_sem=recv_b.at[k],
            device_id={"region": lax.rem(high + k, count) * width + low},
            device_id_type=MESH,
        )

    def across(k, source):
        return pltpu.make_async_remote_copy(
            src_ref=all_ref.at[source],
            dst_ref=all_ref.at[source],
            send_sem=send_c.at[k],
            recv_sem=recv_c.at[k],
            device_id={"region": high * width + 1 - low},
            device_id_type=MESH,
        )

    firsts = [first(k) for k in range(1, regions)]
    for copy in firsts:
        copy.start()

    pair_count = pairs_ref.shape[0]

    def turn(g, carry):
        for j in range(TURNS):
            turned_ref[g * TURNS + j] = turned_pair(pairs_ref[g * TURNS + j])
        return carry

    rounds = pair_count // TURNS
    lax.fori_loop(0, rounds // 2, turn, 0)
    evolved = part_ref[me].astype(F32)
    for k in range(1, regions):
        firsts[k - 1].wait_recv()
        evolved = evolved + got[k].astype(F32)
    misfit = (inv * (evolved - obs)).astype(BF16)
    all_ref[me] = misfit
    seconds = [along(k, me) for k in range(1, count)]
    for copy in seconds:
        copy.start()
    if width == 2:
        seconds.append(across(0, me))
        seconds[-1].start()
    own_ref[...] = lax.dot_general(
        table, misfit, (((0,), (0,)), ((), ())), preferred_element_type=F32
    ).astype(BF16)
    lax.fori_loop(rounds // 2, rounds * 3 // 4, turn, 0)
    for k in range(1, count):
        along(k, at(k, low)).wait_recv()
        if width == 2:
            seconds.append(across(k, at(k, low)))
            seconds[-1].start()
    lax.fori_loop(rounds * 3 // 4, rounds, turn, 0)
    if width == 2:
        for k in range(count):
            across(k, at(k, 1 - low)).wait_recv()
    for copy in firsts + seconds:
        copy.wait_send()


def adjoint_kernel(index_ref, early_ref, late_ref, misfit_ref, own_ref, acc, misfit_out):
    acc[...] = jnp.zeros_like(acc)
    early = early_ref.shape[0]

    def body(left_ref, first, g, carry):
        for j in range(PAIRS):
            pair = g * PAIRS + j
            add_products(index_ref, left_ref[pair], misfit_ref, acc, 2, 3, first + pair)
        return carry

    lax.fori_loop(0, early // PAIRS, functools.partial(body, early_ref, 0), 0)
    lax.fori_loop(0, late_ref.shape[0] // PAIRS, functools.partial(body, late_ref, early), 0)
    misfit_out[...] = own_ref[...]


def gradient_kernel(acc_ref, blend_ref, mix_ref, grad_ref, mine, away, got, send_sem, recv_sem):
    me = lax.axis_index("window")
    other = 1 - me
    slabs, cells, ens = grad_ref.shape
    slices = 2 * slabs
    blocks = cells // BLOCK
    barrier = pltpu.get_barrier_semaphore()
    pl.semaphore_signal(barrier, inc=1, device_id={"window": other}, device_id_type=MESH)
    high, low = spread(blend_ref[...], CELLS_AT_ONCE)
    mix = mix_ref[...]
    pl.semaphore_wait(barrier, 1)

    def send(block):
        return pltpu.make_async_remote_copy(
            src_ref=away.at[block],
            dst_ref=got.at[block],
            send_sem=send_sem.at[block],
            recv_sem=recv_sem.at[block],
            device_id={"window": other},
            device_id_type=MESH,
        )

    def pull(block):
        for within in range(BLOCK // (2 * CELLS_AT_ONCE)):
            sides = []
            for half in range(2):
                start = (2 * within + half) * CELLS_AT_ONCE
                rows = [acc_ref[t * blocks + block, pl.ds(start, CELLS_AT_ONCE), :] for t in range(slices)]
                sides.append(jnp.concatenate(rows, axis=0))
            rhs = jnp.concatenate(sides, axis=1)
            rhs_high = rhs.astype(BF16)
            rhs_low = (rhs - rhs_high.astype(F32)).astype(BF16)
            dims = (((0,), (0,)), ((), ()))
            out = lax.dot_general(high, rhs_high, dims, preferred_element_type=F32)
            out = out + lax.dot_general(low, rhs_high, dims, preferred_element_type=F32)
            out = (out + lax.dot_general(high, rhs_low, dims, preferred_element_type=F32)).astype(BF16)
            for half in range(2):
                start = (2 * within + half) * CELLS_AT_ONCE
                piece = out[:, half * ens : (half + 1) * ens].reshape(slices, CELLS_AT_ONCE, ens)
                first, second = piece[:slabs], piece[slabs:]
                mine[block, :, pl.ds(start, CELLS_AT_ONCE), :] = jnp.where(me == 0, first, second)
                away[block, :, pl.ds(start, CELLS_AT_ONCE), :] = jnp.where(me == 0, second, first)

    def finish(block):
        send(block).wait_recv()
        total = (mine[block].astype(F32) + got[block].astype(F32)).astype(BF16).reshape(slabs * BLOCK, ens)
        grad = jnp.dot(total, mix, preferred_element_type=F32).astype(BF16)
        grad_ref[:, pl.ds(block * BLOCK, BLOCK), :] = grad.reshape(slabs, BLOCK, ens)

    for block in range(blocks):
        pull(block)
        send(block).start()
        if block >= LAG:
            finish(block - LAG)
    for block in range(blocks - LAG, blocks):
        finish(block)
    for block in range(blocks):
        send(block).wait_send()


def vmem():
    return pl.BlockSpec(memory_space=pltpu.VMEM)


def hbm():
    return pl.BlockSpec(memory_space=pltpu.HBM)


def stay(x):
    return pltpu.with_memory_space_constraint(x, pltpu.HBM)


def shards(
    regions,
    flux,
    blend,
    footprints,
    receptor_block,
    cell_block,
    slice_index,
    live_counts,
    observed,
    inv_var,
    prior_mix,
):
    slabs, cells, ens = flux.shape
    slices = blend.shape[0]
    cell_blocks = cells // BLOCK
    panel_total = slices * cell_blocks
    slots = footprints.shape[1]
    rows = observed.shape[1]
    own_blocks = rows // BLOCK
    window_blocks = own_blocks * regions

    panels, raw, index = pl.pallas_call(
        functools.partial(blend_kernel, window_blocks),
        out_shape=(
            jax.ShapeDtypeStruct((slices, cells, ens), BF16),
            jax.ShapeDtypeStruct((slots, BLOCK * BLOCK), BF16),
            jax.ShapeDtypeStruct((4, slots), jnp.int32),
        ),
        in_specs=[hbm()] * 3 + [vmem()] + [hbm()] * 3,
        out_specs=(vmem(), vmem(), vmem()),
        scratch_shapes=[
            pltpu.VMEM((slices, cells, ens), BF16),
            pltpu.VMEM((slices, slices), F32),
            pltpu.VMEM((1, slots), jnp.int32),
            pltpu.VMEM((1, slots), jnp.int32),
            pltpu.VMEM((1, slots), jnp.int32),
            pltpu.SemaphoreType.DMA((4,)),
            pltpu.SemaphoreType.DMA((LOADS,)),
            pltpu.SemaphoreType.DMA((PIECES,)),
            pltpu.SemaphoreType.DMA((PIECES,)),
            pltpu.SemaphoreType.DMA((PIECES,)),
        ],
        compiler_params=pltpu.CompilerParams(collective_id=0, has_side_effects=True, vmem_limit_bytes=24 << 20),
        name="blend_slices",
    )(
        stay(receptor_block),
        stay(cell_block),
        stay(slice_index),
        live_counts,
        stay(blend),
        stay(flux),
        stay(footprints),
    )

    smem = pl.BlockSpec(memory_space=pltpu.SMEM)
    half = jax.ShapeDtypeStruct((slots // 4, BLOCK, 2 * BLOCK), BF16)
    part, early, pairs = pl.pallas_call(
        forward_kernel,
        out_shape=(jax.ShapeDtypeStruct((window_blocks, BLOCK, ens), BF16), half, half),
        in_specs=[smem, vmem(), vmem()],
        out_specs=(vmem(), vmem(), vmem()),
        scratch_shapes=[pltpu.VMEM((window_blocks + 1, BLOCK, ens), F32)],
        compiler_params=pltpu.CompilerParams(vmem_limit_bytes=16 << 20),
        name="forward_blocks",
    )(index, raw, panels.reshape(panel_total, BLOCK, ens))

    misfit_all, own, late = pl.pallas_call(
        functools.partial(exchange_kernel, regions),
        out_shape=(
            jax.ShapeDtypeStruct((regions, rows, ens), BF16),
            jax.ShapeDtypeStruct((rows, ens), BF16),
            half,
        ),
        in_specs=[vmem()] * 4,
        out_specs=(vmem(), vmem(), vmem()),
        scratch_shapes=[
            pltpu.VMEM((regions, rows, ens), BF16),
            pltpu.SemaphoreType.DMA((regions,)),
            pltpu.SemaphoreType.DMA((regions,)),
            pltpu.SemaphoreType.DMA((regions,)),
            pltpu.SemaphoreType.DMA((regions,)),
            pltpu.SemaphoreType.DMA((regions,)),
            pltpu.SemaphoreType.DMA((regions,)),
        ],
        compiler_params=pltpu.CompilerParams(collective_id=1, has_side_effects=True, vmem_limit_bytes=16 << 20),
        name="misfit_exchange",
    )(part.reshape(regions, rows, ens), observed[0], inv_var, pairs)

    collected, misfit = pl.pallas_call(
        adjoint_kernel,
        out_shape=(
            jax.ShapeDtypeStruct((panel_total + 1, BLOCK, ens), F32),
            jax.ShapeDtypeStruct((rows, ens), BF16),
        ),
        in_specs=[smem] + [vmem()] * 4,
        out_specs=(vmem(), vmem()),
        compiler_params=pltpu.CompilerParams(vmem_limit_bytes=16 << 20),
        name="adjoint_blocks",
    )(index, early, late, misfit_all.reshape(window_blocks, BLOCK, ens), own)

    blocks_shape = (cell_blocks, slabs, BLOCK, ens)
    gradient = pl.pallas_call(
        gradient_kernel,
        out_shape=jax.ShapeDtypeStruct((slabs, cells, ens), BF16),
        in_specs=[vmem(), vmem(), vmem()],
        out_specs=vmem(),
        scratch_shapes=[
            pltpu.VMEM(blocks_shape, BF16),
            pltpu.VMEM(blocks_shape, BF16),
            pltpu.VMEM(blocks_shape, BF16),
            pltpu.SemaphoreType.DMA((cell_blocks,)),
            pltpu.SemaphoreType.DMA((cell_blocks,)),
        ],
        compiler_params=pltpu.CompilerParams(collective_id=2, has_side_effects=True, vmem_limit_bytes=16 << 20),
        name="gradient_exchange",
    )(collected, blend, prior_mix)
    return misfit[None], gradient


def solution(mesh):
    in_specs = (
        P(("group", "window"), "region", None),
        P(),
        P(("group", "window"), "region", None),
        P(("group", "window"), "region"),
        P(("group", "window"), "region"),
        P(("group", "window"), "region"),
        P(("group", "window"), "region"),
        P(("group", "window"), "region", None),
        P(("group", "window"), "region"),
        P(),
    )
    out_specs = (P(("group", "window"), "region", None), P(("group", "window"), "region", None))
    return jax.shard_map(
        functools.partial(shards, mesh.shape["region"]),
        mesh=mesh,
        in_specs=in_specs,
        out_specs=out_specs,
        check_vma=False,
    )
```

```python
import functools

import jax
import jax.numpy as jnp
from jax import lax
from jax.experimental import pallas as pl
from jax.experimental.pallas import tpu as pltpu
from jax.sharding import PartitionSpec as P

BLOCK = 64
MESH = pl.DeviceIdType.MESH
F32 = jnp.float32
BF16 = jnp.bfloat16
SUB = 16
SUBS = 4
CELLS_AT_ONCE = 16
PIECES = 4
LOADS = 8
PAIRS = 32
TURNS = 32
LAG = 2


def spread(matrix, width):
    size = matrix.shape[0]
    full = size * width
    row = lax.broadcasted_iota(jnp.int32, (full, size), 0)
    col = lax.broadcasted_iota(jnp.int32, (full, size), 1)
    pick = (row // width == col).astype(BF16)
    row_f = lax.broadcasted_iota(jnp.int32, (full, full), 0)
    col_f = lax.broadcasted_iota(jnp.int32, (full, full), 1)
    same = row_f % width == col_f % width
    high = matrix.astype(BF16)
    low = (matrix - high.astype(F32)).astype(BF16)
    parts = []
    for part in (high, low):
        tall = jnp.dot(pick, part, preferred_element_type=F32).astype(BF16)
        wide = lax.dot_general(tall, pick, (((1,), (1,)), ((), ())), preferred_element_type=F32)
        parts.append(jnp.where(same, wide, 0.0).astype(BF16))
    return parts


def halves_swapped(x):
    return pltpu.roll(x, BLOCK, 1)


def blend_kernel(
    window_blocks,
    recv_hbm,
    cell_hbm,
    slice_hbm,
    live_ref,
    blend_hbm,
    flux_hbm,
    fp_hbm,
    panels_ref,
    pairs_ref,
    index_ref,
    full,
    raw,
    blend_ref,
    recv_ref,
    cell_ref,
    slice_ref,
    small_sem,
    fp_sem,
    local_sem,
    send_sem,
    recv_sem,
):
    me = lax.axis_index("window")
    other = 1 - me
    slabs, cells, ens = flux_hbm.shape
    slices = panels_ref.shape[0]
    slots = raw.shape[0]
    barrier = pltpu.get_barrier_semaphore()
    pl.semaphore_signal(barrier, inc=1, device_id={"window": other}, device_id_type=MESH)
    smalls = [
        pltpu.make_async_copy(source, target, small_sem.at[k])
        for k, (source, target) in enumerate(
            ((blend_hbm, blend_ref), (recv_hbm, recv_ref), (cell_hbm, cell_ref), (slice_hbm, slice_ref))
        )
    ]
    for copy in smalls:
        copy.start()
    piece = cells // PIECES
    locals_, sends, loads = [], [], []
    for k in range(PIECES):
        span = pl.ds(k * piece, piece)
        locals_.append(
            pltpu.make_async_copy(
                flux_hbm.at[:, span, :], full.at[pl.ds(me * slabs, slabs), span, :], local_sem.at[k]
            )
        )
        locals_[-1].start()
    part = slots // LOADS
    for k in range(LOADS):
        span = pl.ds(k * part, part)
        loads.append(pltpu.make_async_copy(fp_hbm.at[0, span, :], raw.at[span, :], fp_sem.at[k]))
    loads[0].start()
    pl.semaphore_wait(barrier, 1)
    for k in range(PIECES):
        span = pl.ds(k * piece, piece)
        sends.append(
            pltpu.make_async_remote_copy(
                src_ref=flux_hbm.at[:, span, :],
                dst_ref=full.at[pl.ds(me * slabs, slabs), span, :],
                send_sem=send_sem.at[k],
                recv_sem=recv_sem.at[k],
                device_id={"window": other},
                device_id_type=MESH,
            )
        )
        sends[-1].start()
    for k in range(1, LOADS):
        loads[k].start()

    for copy in smalls:
        copy.wait()
    cell_blocks = cells // BLOCK
    live = lax.broadcasted_iota(jnp.int32, recv_ref.shape, 1) < live_ref[...]
    panel = slice_ref[...] * cell_blocks + cell_ref[...]
    index_ref[pl.ds(0, 1), :] = jnp.where(live, recv_ref[...], window_blocks)
    index_ref[pl.ds(1, 1), :] = jnp.where(live, panel, 0)
    index_ref[pl.ds(2, 1), :] = jnp.where(live, panel, slices * cell_blocks)
    index_ref[pl.ds(3, 1), :] = jnp.where(live, recv_ref[...], 0)
    high, low = spread(blend_ref[...], CELLS_AT_ONCE)

    def arrange(k):
        loads[k].wait()

        def body(g, carry):
            lower = lax.broadcasted_iota(jnp.int32, (BLOCK // 2, 2 * BLOCK), 1) < BLOCK
            for sub in range(SUBS):
                base = pl.multiple_of(k * part + g * SUBS * SUB + sub * SUB, SUB)
                x = raw[pl.ds(base, SUB), :].reshape(SUB, BLOCK // 2, 2 * BLOCK)
                for j in range(0, SUB, 2):
                    one, two = x[j], x[j + 1]
                    even = jnp.where(lower, one, halves_swapped(two))
                    odd = jnp.where(lower, halves_swapped(one), two)
                    place = k * (part // 2) + (g * SUBS + sub) * (SUB // 2) + j // 2
                    pairs_ref[place] = jnp.concatenate([even, odd], axis=0)
            return carry

        lax.fori_loop(0, part // SUB // SUBS, body, 0)

    for k in range(LOADS // 2):
        arrange(k)
    for k in range(PIECES):
        locals_[k].wait()
        sends[k].wait_recv()

        def group(g, carry, k=k):
            sides = []
            for half in range(2):
                start = pl.multiple_of(k * piece + g * 2 * CELLS_AT_ONCE + half * CELLS_AT_ONCE, CELLS_AT_ONCE)
                sides.append(full[:, pl.ds(start, CELLS_AT_ONCE), :].reshape(slices * CELLS_AT_ONCE, ens))
            rhs = jnp.concatenate(sides, axis=1)
            out = jnp.dot(high, rhs, preferred_element_type=F32) + jnp.dot(low, rhs, preferred_element_type=F32)
            out = out.astype(BF16)
            for half in range(2):
                start = pl.multiple_of(k * piece + g * 2 * CELLS_AT_ONCE + half * CELLS_AT_ONCE, CELLS_AT_ONCE)
                panels_ref[:, pl.ds(start, CELLS_AT_ONCE), :] = out[:, half * ens : (half + 1) * ens].reshape(
                    slices, CELLS_AT_ONCE, ens
                )
            return carry

        lax.fori_loop(0, piece // (2 * CELLS_AT_ONCE), group, 0, unroll=2)
    for k in range(LOADS // 2, LOADS):
        arrange(k)
    for k in range(PIECES):
        sends[k].wait_send()


def both(one, two):
    zero = jnp.zeros_like(one)
    return jnp.concatenate(
        [jnp.concatenate([one, zero], axis=1), jnp.concatenate([zero, two], axis=1)], axis=0
    )


def products(index_ref, left_ref, right_ref, acc, to, source):
    acc[...] = jnp.zeros_like(acc)
    ens = acc.shape[2]

    def body(g, carry):
        for j in range(PAIRS):
            pair = g * PAIRS + j
            one = right_ref[index_ref[source, 2 * pair]]
            two = right_ref[index_ref[source, 2 * pair + 1]]
            out = jnp.dot(left_ref[pair], both(one, two), preferred_element_type=F32)
            acc[index_ref[to, 2 * pair]] += out[:, :ens]
            acc[index_ref[to, 2 * pair + 1]] += out[:, ens:]
        return carry

    lax.fori_loop(0, left_ref.shape[0] // PAIRS, body, 0)


def forward_kernel(index_ref, pairs_ref, panels_ref, part_ref, acc):
    products(index_ref, pairs_ref, panels_ref, acc, 0, 1)
    part_ref[...] = acc[pl.ds(0, part_ref.shape[0])].astype(BF16)


def turned_pair(x):
    t = x.T
    return jnp.concatenate([t[:BLOCK], t[BLOCK:]], axis=1)


def exchange_kernel(
    regions, part_ref, obs_ref, inv_ref, pairs_ref, all_ref, own_ref, turned_ref, got, send_a, recv_a, send_b, recv_b, send_c, recv_c
):
    me = lax.axis_index("region")
    rows, ens = obs_ref.shape
    barrier = pltpu.get_barrier_semaphore()
    for k in range(1, regions):
        peer = lax.rem(me + k, regions)
        pl.semaphore_signal(barrier, inc=1, device_id={"region": peer}, device_id_type=MESH)
    row = lax.broadcasted_iota(jnp.int32, (rows, rows), 0)
    col = lax.broadcasted_iota(jnp.int32, (rows, rows), 1)
    inner = row % BLOCK
    half = BLOCK // 2
    picked = (row // BLOCK) * BLOCK + (inner % half) * 2 + inner // half == col
    table = picked.astype(BF16)
    obs = jnp.dot(table, obs_ref[...], preferred_element_type=F32)
    inv = jnp.sum(jnp.where(picked, inv_ref[...], 0.0), axis=1, keepdims=True)
    pl.semaphore_wait(barrier, regions - 1)

    def first(k):
        peer = lax.rem(me + k, regions)
        return pltpu.make_async_remote_copy(
            src_ref=part_ref.at[peer],
            dst_ref=got.at[k],
            send_sem=send_a.at[k],
            recv_sem=recv_a.at[k],
            device_id={"region": peer},
            device_id_type=MESH,
        )

    width = 2 if regions % 2 == 0 else 1
    count = regions // width
    high, low = me // width, lax.rem(me, width)

    def at(k, low):
        return lax.rem(high + count - k, count) * width + low

    def along(k, source):
        return pltpu.make_async_remote_copy(
            src_ref=all_ref.at[source],
            dst_ref=all_ref.at[source],
            send_sem=send_b.at[k],
            recv_sem=recv_b.at[k],
            device_id={"region": lax.rem(high + k, count) * width + low},
            device_id_type=MESH,
        )

    def across(k, source):
        return pltpu.make_async_remote_copy(
            src_ref=all_ref.at[source],
            dst_ref=all_ref.at[source],
            send_sem=send_c.at[k],
            recv_sem=recv_c.at[k],
            device_id={"region": high * width + 1 - low},
            device_id_type=MESH,
        )

    firsts = [first(k) for k in range(1, regions)]
    for copy in firsts:
        copy.start()

    pair_count = pairs_ref.shape[0]

    def turn(g, carry):
        for j in range(TURNS):
            turned_ref[g * TURNS + j] = turned_pair(pairs_ref[g * TURNS + j])
        return carry

    rounds = pair_count // TURNS
    lax.fori_loop(0, rounds // 2, turn, 0)
    evolved = part_ref[me].astype(F32)
    for k in range(1, regions):
        firsts[k - 1].wait_recv()
        evolved = evolved + got[k].astype(F32)
    misfit = (inv * (evolved - obs)).astype(BF16)
    all_ref[me] = misfit
    seconds = [along(k, me) for k in range(1, count)]
    for copy in seconds:
        copy.start()
    if width == 2:
        seconds.append(across(0, me))
        seconds[-1].start()
    own_ref[...] = lax.dot_general(
        table, misfit, (((0,), (0,)), ((), ())), preferred_element_type=F32
    ).astype(BF16)
    lax.fori_loop(rounds // 2, rounds * 3 // 4, turn, 0)
    for k in range(1, count):
        along(k, at(k, low)).wait_recv()
        if width == 2:
            seconds.append(across(k, at(k, low)))
            seconds[-1].start()
    lax.fori_loop(rounds * 3 // 4, rounds, turn, 0)
    if width == 2:
        for k in range(count):
            across(k, at(k, 1 - low)).wait_recv()
    for copy in firsts + seconds:
        copy.wait_send()


def adjoint_kernel(index_ref, turned_ref, misfit_ref, own_ref, acc, misfit_out):
    products(index_ref, turned_ref, misfit_ref, acc, 2, 3)
    misfit_out[...] = own_ref[...]


def gradient_kernel(acc_ref, blend_ref, mix_ref, grad_ref, mine, away, got, send_sem, recv_sem):
    me = lax.axis_index("window")
    other = 1 - me
    slabs, cells, ens = grad_ref.shape
    slices = 2 * slabs
    blocks = cells // BLOCK
    barrier = pltpu.get_barrier_semaphore()
    pl.semaphore_signal(barrier, inc=1, device_id={"window": other}, device_id_type=MESH)
    high, low = spread(blend_ref[...], CELLS_AT_ONCE)
    mix = mix_ref[...]
    pl.semaphore_wait(barrier, 1)

    def send(block):
        return pltpu.make_async_remote_copy(
            src_ref=away.at[block],
            dst_ref=got.at[block],
            send_sem=send_sem.at[block],
            recv_sem=recv_sem.at[block],
            device_id={"window": other},
            device_id_type=MESH,
        )

    def pull(block):
        for within in range(BLOCK // (2 * CELLS_AT_ONCE)):
            sides = []
            for half in range(2):
                start = (2 * within + half) * CELLS_AT_ONCE
                rows = [acc_ref[t * blocks + block, pl.ds(start, CELLS_AT_ONCE), :] for t in range(slices)]
                sides.append(jnp.concatenate(rows, axis=0))
            rhs = jnp.concatenate(sides, axis=1)
            rhs_high = rhs.astype(BF16)
            rhs_low = (rhs - rhs_high.astype(F32)).astype(BF16)
            dims = (((0,), (0,)), ((), ()))
            out = lax.dot_general(high, rhs_high, dims, preferred_element_type=F32)
            out = out + lax.dot_general(low, rhs_high, dims, preferred_element_type=F32)
            out = (out + lax.dot_general(high, rhs_low, dims, preferred_element_type=F32)).astype(BF16)
            for half in range(2):
                start = (2 * within + half) * CELLS_AT_ONCE
                piece = out[:, half * ens : (half + 1) * ens].reshape(slices, CELLS_AT_ONCE, ens)
                first, second = piece[:slabs], piece[slabs:]
                mine[block, :, pl.ds(start, CELLS_AT_ONCE), :] = jnp.where(me == 0, first, second)
                away[block, :, pl.ds(start, CELLS_AT_ONCE), :] = jnp.where(me == 0, second, first)

    def finish(block):
        send(block).wait_recv()
        total = (mine[block].astype(F32) + got[block].astype(F32)).astype(BF16).reshape(slabs * BLOCK, ens)
        grad = jnp.dot(total, mix, preferred_element_type=F32).astype(BF16)
        grad_ref[:, pl.ds(block * BLOCK, BLOCK), :] = grad.reshape(slabs, BLOCK, ens)

    for block in range(blocks):
        pull(block)
        send(block).start()
        if block >= LAG:
            finish(block - LAG)
    for block in range(blocks - LAG, blocks):
        finish(block)
    for block in range(blocks):
        send(block).wait_send()


def vmem():
    return pl.BlockSpec(memory_space=pltpu.VMEM)


def hbm():
    return pl.BlockSpec(memory_space=pltpu.HBM)


def stay(x):
    return pltpu.with_memory_space_constraint(x, pltpu.HBM)


def shards(
    regions,
    flux,
    blend,
    footprints,
    receptor_block,
    cell_block,
    slice_index,
    live_counts,
    observed,
    inv_var,
    prior_mix,
):
    slabs, cells, ens = flux.shape
    slices = blend.shape[0]
    cell_blocks = cells // BLOCK
    panel_total = slices * cell_blocks
    slots = footprints.shape[1]
    rows = observed.shape[1]
    own_blocks = rows // BLOCK
    window_blocks = own_blocks * regions

    panels, pairs, index = pl.pallas_call(
        functools.partial(blend_kernel, window_blocks),
        out_shape=(
            jax.ShapeDtypeStruct((slices, cells, ens), BF16),
            jax.ShapeDtypeStruct((slots // 2, BLOCK, 2 * BLOCK), BF16),
            jax.ShapeDtypeStruct((4, slots), jnp.int32),
        ),
        in_specs=[hbm()] * 3 + [vmem()] + [hbm()] * 3,
        out_specs=(vmem(), vmem(), vmem()),
        scratch_shapes=[
            pltpu.VMEM((slices, cells, ens), BF16),
            pltpu.VMEM((slots, BLOCK * BLOCK), BF16),
            pltpu.VMEM((slices, slices), F32),
            pltpu.VMEM((1, slots), jnp.int32),
            pltpu.VMEM((1, slots), jnp.int32),
            pltpu.VMEM((1, slots), jnp.int32),
            pltpu.SemaphoreType.DMA((4,)),
            pltpu.SemaphoreType.DMA((LOADS,)),
            pltpu.SemaphoreType.DMA((PIECES,)),
            pltpu.SemaphoreType.DMA((PIECES,)),
            pltpu.SemaphoreType.DMA((PIECES,)),
        ],
        compiler_params=pltpu.CompilerParams(collective_id=0, has_side_effects=True, vmem_limit_bytes=24 << 20),
        name="blend_slices",
    )(
        stay(receptor_block),
        stay(cell_block),
        stay(slice_index),
        live_counts,
        stay(blend),
        stay(flux),
        stay(footprints),
    )

    smem = pl.BlockSpec(memory_space=pltpu.SMEM)
    part = pl.pallas_call(
        forward_kernel,
        out_shape=jax.ShapeDtypeStruct((window_blocks, BLOCK, ens), BF16),
        in_specs=[smem, vmem(), vmem()],
        out_specs=vmem(),
        scratch_shapes=[pltpu.VMEM((window_blocks + 1, BLOCK, ens), F32)],
        compiler_params=pltpu.CompilerParams(vmem_limit_bytes=16 << 20),
        name="forward_blocks",
    )(index, pairs, panels.reshape(panel_total, BLOCK, ens))

    misfit_all, own, turned = pl.pallas_call(
        functools.partial(exchange_kernel, regions),
        out_shape=(
            jax.ShapeDtypeStruct((regions, rows, ens), BF16),
            jax.ShapeDtypeStruct((rows, ens), BF16),
            jax.ShapeDtypeStruct((slots // 2, BLOCK, 2 * BLOCK), BF16),
        ),
        in_specs=[vmem()] * 4,
        out_specs=(vmem(), vmem(), vmem()),
        scratch_shapes=[
            pltpu.VMEM((regions, rows, ens), BF16),
            pltpu.SemaphoreType.DMA((regions,)),
            pltpu.SemaphoreType.DMA((regions,)),
            pltpu.SemaphoreType.DMA((regions,)),
            pltpu.SemaphoreType.DMA((regions,)),
            pltpu.SemaphoreType.DMA((regions,)),
            pltpu.SemaphoreType.DMA((regions,)),
        ],
        compiler_params=pltpu.CompilerParams(collective_id=1, has_side_effects=True, vmem_limit_bytes=16 << 20),
        name="misfit_exchange",
    )(part.reshape(regions, rows, ens), observed[0], inv_var, pairs)

    collected, misfit = pl.pallas_call(
        adjoint_kernel,
        out_shape=(
            jax.ShapeDtypeStruct((panel_total + 1, BLOCK, ens), F32),
            jax.ShapeDtypeStruct((rows, ens), BF16),
        ),
        in_specs=[smem, vmem(), vmem(), vmem()],
        out_specs=(vmem(), vmem()),
        compiler_params=pltpu.CompilerParams(vmem_limit_bytes=16 << 20),
        name="adjoint_blocks",
    )(index, turned, misfit_all.reshape(window_blocks, BLOCK, ens), own)

    blocks_shape = (cell_blocks, slabs, BLOCK, ens)
    gradient = pl.pallas_call(
        gradient_kernel,
        out_shape=jax.ShapeDtypeStruct((slabs, cells, ens), BF16),
        in_specs=[vmem(), vmem(), vmem()],
        out_specs=vmem(),
        scratch_shapes=[
            pltpu.VMEM(blocks_shape, BF16),
            pltpu.VMEM(blocks_shape, BF16),
            pltpu.VMEM(blocks_shape, BF16),
            pltpu.SemaphoreType.DMA((cell_blocks,)),
            pltpu.SemaphoreType.DMA((cell_blocks,)),
        ],
        compiler_params=pltpu.CompilerParams(collective_id=2, has_side_effects=True, vmem_limit_bytes=16 << 20),
        name="gradient_exchange",
    )(collected, blend, prior_mix)
    return misfit[None], gradient


def solution(mesh):
    in_specs = (
        P(("group", "window"), "region", None),
        P(),
        P(("group", "window"), "region", None),
        P(("group", "window"), "region"),
        P(("group", "window"), "region"),
        P(("group", "window"), "region"),
        P(("group", "window"), "region"),
        P(("group", "window"), "region", None),
        P(("group", "window"), "region"),
        P(),
    )
    out_specs = (P(("group", "window"), "region", None), P(("group", "window"), "region", None))
    return jax.shard_map(
        functools.partial(shards, mesh.shape["region"]),
        mesh=mesh,
        in_specs=in_specs,
        out_specs=out_specs,
        check_vma=False,
    )
```
